256 devices in a mesh: ma: 64 (over x, z, core), lev: 4 (over y).
Axes of the slice: x: 4, y: 4, z: 8, core: 2. Of those that a mesh axis runs over, the one named last changes fastest.
Arguments:
- forcing: float32 [72, 2, 1280, 1280], P('lev', None, 'ma'), may hold values from -80 to 80
- coupling: float32 [4, 1280, 1280], P(None, 'ma'), may hold values from -0.3 to 0.3
- helmholtz: float32 [1280], replicated, may hold values from 0.5 to 5
- vertical: float32 [72, 72], replicated, may hold values from -1 to 3, as said below
Outputs:
- solution: float32 [72, 2, 1280, 1280], P('lev', None, 'ma')
- norms: float32 [2], replicated
The draws below stay inside these ranges and needn't reach their ends.
Inputs may be any that keep to these rules, and one draw needn't show every extreme that they name: `vertical`: the diagonal entries lie between 1 and 3.
All inputs are finite; a program needn't handle non-finite values.
Results may differ from the reference program's by a relative error of at most 0.000071.
Values sent between devices are 32-bit elements; how exact they have to be, the bound alone decides.
No kernel may reach another device: no remote copies, remote signals or barrier semaphores. Data moves between devices by JAX's collectives and lax.ppermute only.
A program may use at most 192 MiB of HBM per device.

```python
import math
import jax
import jax.numpy as jnp
from jax import lax

LEV = 72
WAVES = 1280
N_MA = 64


def draw_forcing(key, part):
    base_key, row_key, col_key = jax.random.split(jax.random.fold_in(key, 11), 3)
    shape = (LEV, 2, WAVES, WAVES)
    rows = jnp.arange(WAVES, dtype=jnp.float32)
    ramp = 1.0 + rows / WAVES
    spread = jnp.exp(jax.random.uniform(row_key, (WAVES,), jnp.float32, math.log(0.25), math.log(2.5)))
    columns = jnp.exp(jax.random.uniform(col_key, (WAVES,), jnp.float32, math.log(0.3), math.log(3.0)))
    base = jax.random.truncated_normal(base_key, -4.0, 4.0, shape, jnp.float32)
    return base * (ramp * spread)[None, None, :, None] * columns[None, None, None, :]


def draw_vertical(key, part):
    diag_key, off_key = jax.random.split(jax.random.fold_in(key, 23), 2)
    diagonal = jax.random.uniform(diag_key, (LEV,), jnp.float32, 1.0, 3.0)
    offdiag = jax.random.truncated_normal(off_key, -4.0, 4.0, (LEV, LEV), jnp.float32) / LEV
    identity = jnp.eye(LEV, dtype=jnp.float32)
    return offdiag * (1.0 - identity) + diagonal[None, :] * identity


def block_scale(own_key, shape, cuts, low, largest):
    level, own = 1.0, jax.random.fold_in(own_key, 6)
    for position, shards_of in cuts:
        steps = jnp.exp(jax.random.uniform(jax.random.fold_in(own, position), (shards_of,), jnp.float32, low / len(cuts), largest / len(cuts)))
        level = level * jnp.repeat(steps, shape[position] // shards_of).reshape([-1 if axis == position else 1 for axis in range(len(shape))])
    return level


def setup_inputs(seed: int = 0) -> dict:
    seeds = jax.random.split(jax.random.key(seed), 5)
    return {
        "forcing": draw_forcing(jax.random.fold_in(seeds[4], 71), 0),
        "coupling": jnp.clip(jax.random.uniform(seeds[1], (4, WAVES, WAVES), jnp.float32, -0.3, 0.3) * block_scale(seeds[1], (4, WAVES, WAVES), ((1, 64),), -0.4, 0.0), -0.3, 0.3),
        "helmholtz": jnp.clip(jnp.exp(jax.random.uniform(seeds[2], (WAVES,), jnp.float32, math.log(0.5), math.log(5.0))), 0.5, 5.0),
        "vertical": draw_vertical(jax.random.fold_in(seeds[4], 71), 0),
    }


OFFSETS = (-2, -1, 1, 2)

def storage_waves():
    per_owner = WAVES // N_MA
    place = jnp.arange(WAVES, dtype=jnp.int32)
    owner = place // per_owner
    fold = place % per_owner
    return fold * N_MA + jnp.where(fold % 2 == 0, owner, N_MA - 1 - owner)

def reference(forcing, coupling, helmholtz, vertical):
    waves = storage_waves()
    row_of_wave = jnp.argsort(waves).astype(jnp.int32)
    positions = jnp.arange(WAVES, dtype=jnp.int32)
    live = (positions[None, :] >= waves[:, None]).astype(jnp.float32)[None, None]
    scale = 1.0 / (1.0 + helmholtz[None, :] * jnp.diagonal(vertical)[:, None])
    scale = scale[:, None, None, :]

    def operator(values):
        mixed = jnp.einsum('kl,lcin->kcin', vertical, values, precision=lax.Precision.HIGHEST)
        result = values + helmholtz[None, None, None, :] * mixed
        for place, offset in enumerate(OFFSETS):
            target = waves + offset
            valid = ((target >= 0) & (target < WAVES)).astype(jnp.float32)
            source = row_of_wave[jnp.clip(target, 0, WAVES - 1)].astype(jnp.int32)
            moved = jnp.take(values, source, axis=2) * valid[None, None, :, None]
            result = result + coupling[place][None, None] * moved
        return result * live
    rhs = forcing * live
    first = scale * rhs
    residual = rhs - operator(first)
    solution = first + scale * residual
    count = LEV * WAVES * (WAVES + 1)
    sums = jnp.stack([jnp.sum(rhs * rhs), jnp.sum(residual * residual)])
    norms = jnp.sqrt(sums / count)
    return (solution, norms)
```

```python
import jax
import jax.numpy as jnp
from jax import lax
from jax.experimental import pallas as pl
from jax.experimental.pallas import tpu as pltpu
from jax.sharding import Mesh
from jax.sharding import PartitionSpec as P

LEV = 72
WAVES = 1280
OWNERS = 64
FOLDS = 20
TILES = 10
HALF = 112
QROWS = 56
OWN = 18
MA = ("ma_0", "ma_1", "ma_2")
F32 = jnp.float32


def start_row(t):
    return 20 * t - t * (t - 1)


def cut(moves):
    out = []
    for s, d, n in moves:
        while n:
            step = min(n, QROWS - d % QROWS, QROWS - s % QROWS)
            out.append((s, d, step))
            s, d, n = s + step, d + step, n - step
    return out


def cut_target(moves):
    out = []
    for s, d, n in moves:
        while n:
            step = min(n, QROWS - d % QROWS)
            out.append((s, d, step))
            s, d, n = s + step, d + step, n - step
    return out


PACK = cut_target(
    [((2 * t + par) * 20 + 2 * t, par * HALF + start_row(t), 20 - 2 * t) for par in range(2) for t in range(TILES)]
)
PACK_UP = [(s, (d + HALF) % (2 * HALF), n) for s, d, n in PACK]
PACK_DOWN = cut_target(
    [((2 * t + 2) * 20 + 2 * t + 2, HALF + start_row(t) + 2, 18 - 2 * t) for t in range(TILES - 1)]
    + [((2 * t - 1) * 20 + 2 * t, start_row(t), 20 - 2 * t) for t in range(1, TILES)]
)
DOWN_EMPTY = cut_target(
    [(0, HALF + start_row(t), 2) for t in range(TILES)] + [(0, 0, 20)]
)
PADS = [(0, 110, 2), (0, 222, 2)]


def pack_kernel(step_levels, info, x_ref, p_ref, px_ref, py_ref):
    def fill(ref, moves, empty):
        for l in range(step_levels):
            for s, d, n in moves:
                ref[d // QROWS, l, d % QROWS : d % QROWS + n, :] = x_ref[l, s : s + n, :]
            for _, d, n in empty:
                ref[d // QROWS, l, d % QROWS : d % QROWS + n, :] = jnp.zeros((n, 128), F32)

    fill(p_ref, PACK, PADS)
    for ref, slot in ((px_ref, 0), (py_ref, 1)):
        mode = info[slot]

        @pl.when(mode == 0)
        def _(ref=ref):
            fill(ref, PACK, PADS)

        @pl.when(mode == 1)
        def _(ref=ref):
            fill(ref, PACK_UP, PADS)

        @pl.when(mode == 2)
        def _(ref=ref):
            fill(ref, PACK_DOWN, DOWN_EMPTY + PADS)


def pack(info, x):
    tl = 3
    out = jax.ShapeDtypeStruct((4, OWN, QROWS, 128), F32)
    spec = pl.BlockSpec((4, tl, QROWS, 128), lambda i, s: (0, i, 0, 0))
    return pl.pallas_call(
        lambda *refs: pack_kernel(tl, *refs),
        out_shape=(out, out, out),
        grid_spec=pltpu.PrefetchScalarGridSpec(
            num_scalar_prefetch=1,
            grid=(OWN // tl,),
            in_specs=[pl.BlockSpec((tl, 400, 128), lambda i, s: (i, 0, 0))],
            out_specs=[spec, spec, spec],
        ),
        name="pack",
    )(info, x)


BASES = (1, 2, -2, -1)
PLACE = {-2: 0, -1: 1, 1: 2, 2: 3}


def prep_kernel(info, c_ref, h_ref, ck_ref, hp_ref, live_ref):
    owner = info[2]
    odd = info[3]
    for par in range(2):
        for t in range(TILES):
            fold = 2 * t + par
            n = TILES - t
            at = par * HALF + start_row(t)
            wave = fold * OWNERS + (owner if par == 0 else OWNERS - 1 - owner)
            col = lax.broadcasted_iota(jnp.int32, (n, 128), 0) * 128 + lax.broadcasted_iota(jnp.int32, (n, 128), 1) + 128 * t
            live = jnp.where(col >= wave, 1.0, 0.0).astype(F32)
            h = h_ref[t:TILES, :]
            for part in range(2):
                live_ref[pl.ds(at + part, n, stride=2), :] = live
                hp_ref[pl.ds(at + part, n, stride=2), :] = h
            for a, base in enumerate(BASES):
                s_even = base * (1 if par == 0 else -1)
                shift = jnp.where(odd == 1, -s_even, s_even)
                place = jnp.where(odd == 1, PLACE[-s_even], PLACE[s_even])
                low = jnp.where(wave + shift < 0, 2 * WAVES, jnp.maximum(wave, wave + shift))
                c = c_ref[pl.ds((fold * TILES + t) * 4 + place, n, stride=4), :]
                c = jnp.where(col >= low, c, 0.0)
                for part in range(2):
                    ck_ref[a, pl.ds(at + part, n, stride=2), :] = c
        pad = pl.ds(par * HALF + 110, 2)
        zero = jnp.zeros((2, 128), F32)
        live_ref[pad, :] = zero
        hp_ref[pad, :] = zero
        for a in range(4):
            ck_ref[a, pad, :] = zero


def prep(info, c, h):
    rows = jax.ShapeDtypeStruct((2 * HALF, 128), F32)
    vmem = pl.BlockSpec(memory_space=pltpu.VMEM)
    return pl.pallas_call(
        prep_kernel,
        out_shape=(jax.ShapeDtypeStruct((4, 2 * HALF, 128), F32), rows, rows),
        in_specs=[pl.BlockSpec(memory_space=pltpu.SMEM), vmem, vmem],
        out_specs=(vmem, vmem, vmem),
        name="prep",
    )(info, c, h)


def mix_kernel(info, w_ref, d_ref, h_ref, x_ref, o_ref):
    w = w_ref[...].astype(jnp.bfloat16)
    d = d_ref[...]
    x2 = x_ref.reshape(LEV * 8, 128)
    o2 = o_ref.reshape(LEV * 8, 128)
    for r in range(0, 8, 2):
        highs, lows = [], []
        for e in range(2):
            h = h_ref[0, r + e : r + e + 1, :]
            x = x2[pl.ds(r + e, LEV, stride=8), :]
            f = x * (1.0 / (1.0 + h * d))
            high = f.astype(jnp.bfloat16).astype(F32)
            highs.append(high)
            lows.append(f - high)
        high = jnp.concatenate(highs, axis=1)
        low = jnp.concatenate(lows, axis=1)
        both = jnp.concatenate([high, high, low], axis=0).astype(jnp.bfloat16)
        out = jnp.dot(w, both, preferred_element_type=F32)
        for e in range(2):
            h = h_ref[0, r + e : r + e + 1, :]
            o2[pl.ds(r + e, LEV, stride=8), :] = out[:, e * 128 : (e + 1) * 128] * h


def mix(info, w3, diag, hp, x):
    return pl.pallas_call(
        mix_kernel,
        out_shape=jax.ShapeDtypeStruct((LEV, QROWS, 128), F32),
        grid_spec=pltpu.PrefetchScalarGridSpec(
            num_scalar_prefetch=1,
            grid=(QROWS // 8,),
            in_specs=[
                pl.BlockSpec((LEV, 3 * LEV), lambda i, s: (0, 0)),
                pl.BlockSpec((LEV, 1), lambda i, s: (0, 0)),
                pl.BlockSpec((1, 8, 128), lambda i, s: (s[4], i, 0)),
                pl.BlockSpec((LEV, 8, 128), lambda i, s: (0, i, 0)),
            ],
            out_specs=pl.BlockSpec((LEV, 8, 128), lambda i, s: (0, i, 0)),
        ),
        name="mix",
    )(info, w3, diag, hp, x)


def last_kernel(tl, info, d_ref, ck_ref, hp_ref, live_ref, p_ref, q_ref, x_ref, y_ref, z_ref, m_ref, o_ref, s_ref, buf, acc):
    step = pl.program_id(0)

    @pl.when(step == 0)
    def _():
        acc[...] = jnp.zeros_like(acc)

    for l in range(tl):
        d = d_ref[info[4] * OWN + step * tl + l]
        for q in range(4):
            live = live_ref[q]
            v = p_ref[q, l] * live
            scale = 1.0 / (1.0 + hp_ref[q] * d)
            near = ck_ref[0, q] * q_ref[q, l] + ck_ref[1, q] * x_ref[q, l]
            near = near + ck_ref[2, q] * y_ref[q, l] + ck_ref[3, q] * z_ref[q, l]
            first = scale * v
            residual = v - (first + m_ref[q, l] + scale * near) * live
            buf[l, q * QROWS : (q + 1) * QROWS, :] = first + scale * residual
            acc[0] += jnp.sum((v * v).reshape(QROWS // 8, 8, 128), axis=0)
            acc[1] += jnp.sum((residual * residual).reshape(QROWS // 8, 8, 128), axis=0)
        for par in range(2):
            for t in range(TILES):
                at = (2 * t + par) * 20
                if t:
                    o_ref[l, at : at + 2 * t, :] = jnp.zeros((2 * t, 128), F32)
                n = 20 - 2 * t
                s = par * HALF + start_row(t)
                o_ref[l, at + 2 * t : at + 20, :] = buf[l, s : s + n, :]

    @pl.when(step == pl.num_programs(0) - 1)
    def _():
        row = lax.broadcasted_iota(jnp.int32, (8, 128), 0)
        s_ref[...] = jnp.where(row == 0, jnp.sum(acc[0]), jnp.sum(acc[1]))


def last(info, diag, ck, hp, live, p, q, x, y, z, m):
    tl = 3
    whole = lambda shape: pl.BlockSpec(shape, lambda i, s: (0,) * len(shape))
    block = pl.BlockSpec((4, tl, QROWS, 128), lambda i, s: (0, i, 0, 0))
    return pl.pallas_call(
        lambda *refs: last_kernel(tl, *refs),
        out_shape=(jax.ShapeDtypeStruct((OWN, 400, 128), F32), jax.ShapeDtypeStruct((8, 128), F32)),
        grid_spec=pltpu.PrefetchScalarGridSpec(
            num_scalar_prefetch=1,
            grid=(OWN // tl,),
            in_specs=[
                pl.BlockSpec(memory_space=pltpu.SMEM),
                whole((4, 4, QROWS, 128)),
                whole((4, QROWS, 128)),
                whole((4, QROWS, 128)),
            ]
            + [block] * 6,
            out_specs=[pl.BlockSpec((tl, 400, 128), lambda i, s: (i, 0, 0)), whole((8, 128))],
            scratch_shapes=[pltpu.VMEM((tl, 2 * HALF, 128), F32), pltpu.VMEM((2, 8, 128), F32)],
        ),
        name="last",
    )(info, diag, ck, hp, live, p, q, x, y, z, m)


def routes(owners):
    x, y = [], []
    for o in range(owners):
        down = o - 2 if o >= 2 else 1 - o
        up = o + 2 if o + 2 < owners else 2 * owners - 1 - (o + 2)
        x.append((o, down if o % 2 == 0 else up))
        y.append((o, up if o % 2 == 0 else down))
    return x, y, [(o, o ^ 1) for o in range(owners)]


def total(value, axes):
    n = lax.axis_size(axes)
    every = lax.all_to_all(jnp.broadcast_to(value[None], (n,) + value.shape), axes, 0, 0, tiled=True)
    return jnp.sum(every, axis=0)


def body(forcing, coupling, helmholtz, vertical):
    owner = lax.axis_index(MA).astype(jnp.int32)
    lev = lax.axis_index("lev").astype(jnp.int32)
    odd = owner % 2
    mode_x = jnp.where(owner == 0, 2, jnp.where(owner == OWNERS - 1, 1, 0))
    mode_y = jnp.where(owner == 1, 2, jnp.where(owner == OWNERS - 2, 1, 0))
    info = jnp.stack([mode_x, mode_y, owner, odd, lev]).astype(jnp.int32)
    native = forcing.reshape(OWN, 2, FOLDS, TILES, 128).transpose(0, 2, 3, 1, 4).reshape(OWN, 400, 128)
    crows = coupling.reshape(4, FOLDS, TILES, 128).transpose(1, 2, 0, 3).reshape(800, 128)
    p, px, py = pack(info, native)
    to_x, to_y, swap = routes(OWNERS)
    every = lax.all_to_all(p, "lev", 0, 0, tiled=True).reshape(LEV, QROWS, 128)
    x = lax.ppermute(px, MA, to_x)
    y = lax.ppermute(py, MA, to_y)
    q = lax.ppermute(p, MA, swap)
    ck, hp, live = prep(info, crows, helmholtz.reshape(TILES, 128))
    ck = ck.reshape(4, 4, QROWS, 128)
    hp = hp.reshape(4, QROWS, 128)
    live = live.reshape(4, QROWS, 128)
    diag = jnp.sum(vertical * jnp.eye(LEV, dtype=F32), axis=1)
    high = lax.reduce_precision(vertical, 8, 7)
    w3 = jnp.concatenate([high, vertical - high, high], axis=1)
    m = mix(info, w3, diag[:, None], hp, every).reshape(4, OWN, QROWS, 128)
    m = lax.all_to_all(m, "lev", 0, 0, tiled=True)
    z = lax.ppermute(x, MA, swap)
    rows, sums = last(info, diag, ck, hp, live, p, q, x, y, z, m)
    solution = rows.reshape(OWN, FOLDS, TILES, 2, 128).transpose(0, 3, 1, 2, 4).reshape(OWN, 2, FOLDS, WAVES)
    sums = total(total(sums, ("ma_1", "ma_2")), ("ma_0", "lev"))
    norms = jnp.sqrt(sums[:2, 0] / (LEV * WAVES * (WAVES + 1)))
    return (solution, norms)


def solution(mesh):
    split = Mesh(mesh.devices.reshape(4, 8, 2, mesh.shape["lev"]), ("ma_0", "ma_1", "ma_2", "lev"))
    return jax.shard_map(
        body,
        mesh=split,
        in_specs=(P("lev", None, MA, None), P(None, MA, None), P(), P()),
        out_specs=(P("lev", None, MA, None), P()),
        check_vma=False,
    )
```

```python
import jax
import jax.numpy as jnp
from jax import lax
from jax.experimental import pallas as pl
from jax.experimental.pallas import tpu as pltpu
from jax.sharding import Mesh
from jax.sharding import PartitionSpec as P

LEV = 72
WAVES = 1280
OWNERS = 64
FOLDS = 20
TILES = 10
HALF = 112
QROWS = 56
OWN = 18
MA = ("ma_0", "ma_1", "ma_2")
F32 = jnp.float32


def start_row(t):
    return 20 * t - t * (t - 1)


def cut(moves):
    out = []
    for s, d, n in moves:
        while n:
            step = min(n, QROWS - d % QROWS, QROWS - s % QROWS)
            out.append((s, d, step))
            s, d, n = s + step, d + step, n - step
    return out


LIVE = [
    (2 * t + par, j, par * HALF + start_row(t) + 2 * (j - t)) for par in range(2) for t in range(TILES) for j in range(t, TILES)
]
DOWN = cut(
    [(start_row(t + 1), HALF + start_row(t) + 2, 18 - 2 * t) for t in range(TILES - 1)]
    + [(HALF + start_row(t - 1) + 2, start_row(t), 20 - 2 * t) for t in range(1, TILES)]
)


def pack_kernel(x_ref, p_ref):
    for fold, j, row in LIVE:
        q, r = divmod(row, QROWS)
        p_ref[q, :, r : r + 2, :] = x_ref[:, fold, :, 128 * j : 128 * j + 128]
    for q in (1, 3):
        p_ref[q, :, QROWS - 2 :, :] = jnp.zeros((p_ref.shape[1], 2, 128), F32)


def pack(x):
    tl = 3
    return pl.pallas_call(
        pack_kernel,
        out_shape=jax.ShapeDtypeStruct((4, OWN, QROWS, 128), F32),
        grid=(OWN // tl,),
        in_specs=[pl.BlockSpec((tl, FOLDS, 2, WAVES), lambda i: (i, 0, 0, 0))],
        out_specs=pl.BlockSpec((4, tl, QROWS, 128), lambda i: (0, i, 0, 0)),
        name="pack",
    )(x)


BASES = (1, 2, -2, -1)
PLACE = {-2: 0, -1: 1, 1: 2, 2: 3}


def prep_kernel(info, c_ref, h_ref, ck_ref, hp_ref, live_ref):
    owner = info[0]
    odd = info[1]
    for par in range(2):
        for t in range(TILES):
            fold = 2 * t + par
            n = TILES - t
            at = par * HALF + start_row(t)
            wave = fold * OWNERS + (owner if par == 0 else OWNERS - 1 - owner)
            col = lax.broadcasted_iota(jnp.int32, (n, 128), 0) * 128 + lax.broadcasted_iota(jnp.int32, (n, 128), 1) + 128 * t
            live = jnp.where(col >= wave, 1.0, 0.0).astype(F32)
            h = h_ref[t:TILES, :]
            for part in range(2):
                live_ref[pl.ds(at + part, n, stride=2), :] = live
                hp_ref[pl.ds(at + part, n, stride=2), :] = h
            for a, base in enumerate(BASES):
                s_even = base * (1 if par == 0 else -1)
                shift = jnp.where(odd == 1, -s_even, s_even)
                place = jnp.where(odd == 1, PLACE[-s_even], PLACE[s_even])
                low = jnp.where(wave + shift < 0, 2 * WAVES, jnp.maximum(wave, wave + shift))
                c = c_ref[pl.ds((fold * TILES + t) * 4 + place, n, stride=4), :]
                c = jnp.where(col >= low, c, 0.0)
                for part in range(2):
                    ck_ref[a, pl.ds(at + part, n, stride=2), :] = c
        pad = pl.ds(par * HALF + 110, 2)
        zero = jnp.zeros((2, 128), F32)
        live_ref[pad, :] = zero
        hp_ref[pad, :] = zero
        for a in range(4):
            ck_ref[a, pad, :] = zero


def prep(info, c, h):
    rows = jax.ShapeDtypeStruct((2 * HALF, 128), F32)
    vmem = pl.BlockSpec(memory_space=pltpu.VMEM)
    return pl.pallas_call(
        prep_kernel,
        out_shape=(jax.ShapeDtypeStruct((4, 2 * HALF, 128), F32), rows, rows),
        in_specs=[pl.BlockSpec(memory_space=pltpu.SMEM), vmem, vmem],
        out_specs=(vmem, vmem, vmem),
        name="prep",
    )(info, c, h)


def mix_kernel(info, w_ref, d_ref, h_ref, x_ref, o_ref):
    w = w_ref[...].astype(jnp.bfloat16)
    d = d_ref[...]
    x2 = x_ref.reshape(LEV * 8, 128)
    o2 = o_ref.reshape(LEV * 8, 128)
    for r in range(0, 8, 2):
        h = h_ref[0, r : r + 1, :]
        scale = 1.0 / (1.0 + h * d)
        highs, lows = [], []
        for e in range(2):
            f = x2[pl.ds(r + e, LEV, stride=8), :] * scale
            high = f.astype(jnp.bfloat16).astype(F32)
            highs.append(high)
            lows.append(f - high)
        high = jnp.concatenate(highs, axis=1)
        low = jnp.concatenate(lows, axis=1)
        both = jnp.concatenate([high, high, low], axis=0).astype(jnp.bfloat16)
        out = jnp.dot(w, both, preferred_element_type=F32)
        for e in range(2):
            o2[pl.ds(r + e, LEV, stride=8), :] = out[:, e * 128 : (e + 1) * 128] * h


def mix(info, w3, diag, hp, x):
    return pl.pallas_call(
        mix_kernel,
        out_shape=jax.ShapeDtypeStruct((LEV, QROWS, 128), F32),
        grid_spec=pltpu.PrefetchScalarGridSpec(
            num_scalar_prefetch=1,
            grid=(QROWS // 8,),
            in_specs=[
                pl.BlockSpec((LEV, 3 * LEV), lambda i, s: (0, 0)),
                pl.BlockSpec((LEV, 1), lambda i, s: (0, 0)),
                pl.BlockSpec((1, 8, 128), lambda i, s: (s[2], i, 0)),
                pl.BlockSpec((LEV, 8, 128), lambda i, s: (0, i, 0)),
            ],
            out_specs=pl.BlockSpec((LEV, 8, 128), lambda i, s: (0, i, 0)),
        ),
        name="mix",
    )(info, w3, diag, hp, x)


def fold_sum(acc, slot, value):
    acc[slot] += jnp.sum((value * value).reshape(QROWS // 8, 8, 128), axis=0)


def near_kernel(tl, info, d_ref, ck_ref, hp_ref, live_ref, p_ref, q_ref, x_ref, y_ref, z_ref, o_ref, s_ref, fix):
    step = pl.program_id(0)
    received = (x_ref, y_ref, z_ref)

    @pl.when(step == 0)
    def _():
        s_ref[...] = jnp.zeros_like(s_ref)
        fix[...] = jnp.zeros_like(fix)

    def one(l, get):
        d = d_ref[info[2] * OWN + step * tl + l]
        for q in range(4):
            live = live_ref[q]
            v = p_ref[q, l] * live
            scale = 1.0 / (1.0 + hp_ref[q] * d)
            near = ck_ref[0, q] * q_ref[q, l] + v
            for a in range(3):
                near = near + ck_ref[a + 1, q] * get(a, q)
            o_ref[q, l] = v - scale * near * live
            fold_sum(s_ref, 0, v)

    @pl.when(info[0] > 1)
    def _():
        def level(l, _):
            one(l, lambda a, q: received[a][jnp.where(info[3 + a] == 1, q ^ 2, q), l])
            return 0

        lax.fori_loop(0, tl, level, 0)

    @pl.when(info[0] <= 1)
    def _():
        def level(l, _):
            for a in range(3):

                @pl.when(info[3 + a] == 2)
                def _():
                    for s, t, n in DOWN:
                        fix[a, t // QROWS, t % QROWS : t % QROWS + n, :] = received[a][s // QROWS, l, s % QROWS : s % QROWS + n, :]

                @pl.when(info[3 + a] != 2)
                def _():
                    fix[a] = received[a][:, l]

            one(l, lambda a, q: fix[a, q])
            return 0

        lax.fori_loop(0, tl, level, 0)


def whole(shape):
    return pl.BlockSpec(shape, lambda i, s: (0,) * len(shape))


def near(info, diag, ck, hp, live, p, q, x, y, z):
    tl = 3
    block = pl.BlockSpec((4, tl, QROWS, 128), lambda i, s: (0, i, 0, 0))
    return pl.pallas_call(
        lambda *refs: near_kernel(tl, *refs),
        out_shape=(jax.ShapeDtypeStruct((4, OWN, QROWS, 128), F32), jax.ShapeDtypeStruct((1, 8, 128), F32)),
        grid_spec=pltpu.PrefetchScalarGridSpec(
            num_scalar_prefetch=1,
            grid=(OWN // tl,),
            in_specs=[
                pl.BlockSpec(memory_space=pltpu.SMEM),
                whole((4, 4, QROWS, 128)),
                whole((4, QROWS, 128)),
                whole((4, QROWS, 128)),
            ]
            + [block] * 5,
            out_specs=[block, whole((1, 8, 128))],
            scratch_shapes=[pltpu.VMEM((3, 4, QROWS, 128), F32)],
        ),
        name="near",
    )(info, diag, ck, hp, live, p, q, x, y, z)


def last_kernel(tl, info, d_ref, v_sum, hp_ref, live_ref, p_ref, part_ref, m_ref, o_ref, s_ref, buf, acc):
    step = pl.program_id(0)

    @pl.when(step == 0)
    def _():
        acc[...] = jnp.zeros_like(acc)

    for l in range(tl):
        d = d_ref[info[2] * OWN + step * tl + l]
        for q in range(4):
            live = live_ref[q]
            scale = 1.0 / (1.0 + hp_ref[q] * d)
            residual = part_ref[q, l] - m_ref[q, l] * live
            buf[l, q * QROWS : (q + 1) * QROWS, :] = scale * (p_ref[q, l] * live + residual)
            fold_sum(acc, 0, residual)
    for t in range(1, TILES):
        for par in range(2):
            o_ref[:, 2 * t + par, :, : 128 * t] = jnp.zeros((tl, 2, 128 * t), F32)
    for fold, j, row in LIVE:
        o_ref[:, fold, :, 128 * j : 128 * j + 128] = buf[:, row : row + 2, :]

    @pl.when(step == pl.num_programs(0) - 1)
    def _():
        row = lax.broadcasted_iota(jnp.int32, (8, 128), 0)
        s_ref[...] = jnp.where(row == 0, jnp.sum(v_sum[0]), jnp.sum(acc[0]))


def last(info, diag, v_sum, hp, live, p, part, m):
    tl = 3
    block = pl.BlockSpec((4, tl, QROWS, 128), lambda i, s: (0, i, 0, 0))
    return pl.pallas_call(
        lambda *refs: last_kernel(tl, *refs),
        out_shape=(jax.ShapeDtypeStruct((OWN, FOLDS, 2, WAVES), F32), jax.ShapeDtypeStruct((8, 128), F32)),
        grid_spec=pltpu.PrefetchScalarGridSpec(
            num_scalar_prefetch=1,
            grid=(OWN // tl,),
            in_specs=[
                pl.BlockSpec(memory_space=pltpu.SMEM),
                whole((1, 8, 128)),
                whole((4, QROWS, 128)),
                whole((4, QROWS, 128)),
            ]
            + [block] * 3,
            out_specs=[pl.BlockSpec((tl, FOLDS, 2, WAVES), lambda i, s: (i, 0, 0, 0)), whole((8, 128))],
            scratch_shapes=[pltpu.VMEM((tl, 2 * HALF, 128), F32), pltpu.VMEM((1, 8, 128), F32)],
        ),
        name="last",
    )(info, diag, v_sum, hp, live, p, part, m)


def routes(owners):
    x, y = [], []
    for o in range(owners):
        down = o - 2 if o >= 2 else 1 - o
        up = o + 2 if o + 2 < owners else 2 * owners - 1 - (o + 2)
        x.append((o, down if o % 2 == 0 else up))
        y.append((o, up if o % 2 == 0 else down))
    return x, y, [(o, o ^ 1) for o in range(owners)]


def total(value, axes):
    n = lax.axis_size(axes)
    every = lax.all_to_all(jnp.broadcast_to(value[None], (n,) + value.shape), axes, 0, 0, tiled=True)
    return jnp.sum(every, axis=0)


def body(forcing, coupling, helmholtz, vertical):
    owner = lax.axis_index(MA).astype(jnp.int32)
    lev = lax.axis_index("lev").astype(jnp.int32)
    ends = {"x": (1, OWNERS - 2), "y": (0, OWNERS - 1), "z": (0, OWNERS - 1)}
    modes = [jnp.where(owner == low, 2, jnp.where(owner == high, 1, 0)) for low, high in ends.values()]
    info = jnp.stack([owner, owner & 1, lev] + modes).astype(jnp.int32)
    crows = coupling.reshape(4, FOLDS, TILES, 128).transpose(1, 2, 0, 3).reshape(800, 128)
    p = pack(forcing.transpose(0, 2, 1, 3))
    to_x, to_y, swap = routes(OWNERS)
    every = lax.all_to_all(p, "lev", 0, 0, tiled=True).reshape(LEV, QROWS, 128)
    x = lax.ppermute(p, MA, to_x)
    y = lax.ppermute(p, MA, to_y)
    q = lax.ppermute(p, MA, swap)
    ck, hp, live = prep(info, crows, helmholtz.reshape(TILES, 128))
    ck = ck.reshape(4, 4, QROWS, 128)
    hp = hp.reshape(4, QROWS, 128)
    live = live.reshape(4, QROWS, 128)
    diag = jnp.sum(vertical * jnp.eye(LEV, dtype=F32), axis=1)
    high = lax.reduce_precision(vertical, 8, 7)
    w3 = jnp.concatenate([high, vertical - high, high], axis=1)
    m = mix(info, w3, diag[:, None], hp, every).reshape(4, OWN, QROWS, 128)
    x, m = lax.optimization_barrier((x, m))
    m = lax.all_to_all(m, "lev", 0, 0, tiled=True)
    z = lax.ppermute(x, MA, swap)
    part, v_sum = near(info, diag, ck, hp, live, p, q, x, y, z)
    part, m = lax.optimization_barrier((part, m))
    rows, sums = last(info, diag, v_sum, hp, live, p, part, m)
    sums = total(total(sums, ("ma_1", "ma_2")), ("ma_0", "lev"))
    norms = jnp.sqrt(sums[:2, 0] / (LEV * WAVES * (WAVES + 1)))
    return (rows.transpose(0, 2, 1, 3), norms)


def solution(mesh):
    split = Mesh(mesh.devices.reshape(4, 8, 2, mesh.shape["lev"]), ("ma_0", "ma_1", "ma_2", "lev"))
    return jax.shard_map(
        body,
        mesh=split,
        in_specs=(P("lev", None, MA, None), P(None, MA, None), P(), P()),
        out_specs=(P("lev", None, MA, None), P()),
        check_vma=False,
    )
```

```python
import jax
import jax.numpy as jnp
from jax import lax
from jax.experimental import pallas as pl
from jax.experimental.pallas import tpu as pltpu
from jax.sharding import Mesh
from jax.sharding import PartitionSpec as P

LEV = 72
WAVES = 1280
OWNERS = 64
FOLDS = 20
TILES = 10
HALF = 112
QROWS = 56
OWN = 18
STEP = 3
MA = ("ma_0", "ma_1", "ma_2")
F32 = jnp.float32


def start_row(t):
    return 20 * t - t * (t - 1)


def cut(moves):
    out = []
    for s, d, n in moves:
        while n:
            step = min(n, QROWS - d % QROWS, QROWS - s % QROWS)
            out.append((s, d, step))
            s, d, n = s + step, d + step, n - step
    return out


LIVE = [
    (2 * t + par, j, par * HALF + start_row(t) + 2 * (j - t)) for par in range(2) for t in range(TILES) for j in range(t, TILES)
]
DOWN = cut(
    [(start_row(t + 1), HALF + start_row(t) + 2, 18 - 2 * t) for t in range(TILES - 1)]
    + [(HALF + start_row(t - 1) + 2, start_row(t), 20 - 2 * t) for t in range(1, TILES)]
)


def pack_kernel(x_ref, p_ref):
    for fold, j, row in LIVE:
        q, r = divmod(row, QROWS)
        p_ref[q, :, r : r + 2, :] = x_ref[:, fold, :, 128 * j : 128 * j + 128]
    for q in (1, 3):
        p_ref[q, :, QROWS - 2 :, :] = jnp.zeros((p_ref.shape[1], 2, 128), F32)


def pack(x):
    return pl.pallas_call(
        pack_kernel,
        out_shape=jax.ShapeDtypeStruct((4, OWN, QROWS, 128), F32),
        grid=(OWN // STEP,),
        in_specs=[pl.BlockSpec((STEP, FOLDS, 2, WAVES), lambda i: (i, 0, 0, 0))],
        out_specs=pl.BlockSpec((4, STEP, QROWS, 128), lambda i: (0, i, 0, 0)),
        name="pack",
    )(x)


BASES = (1, 2, -2, -1)
PLACE = {-2: 0, -1: 1, 1: 2, 2: 3}


def prep_kernel(info, c_ref, h_ref, ck_ref, hp_ref, live_ref):
    owner = info[0]
    odd = info[1]
    for par in range(2):
        for t in range(TILES):
            fold = 2 * t + par
            n = TILES - t
            at = par * HALF + start_row(t)
            wave = fold * OWNERS + (owner if par == 0 else OWNERS - 1 - owner)
            col = lax.broadcasted_iota(jnp.int32, (n, 128), 0) * 128 + lax.broadcasted_iota(jnp.int32, (n, 128), 1) + 128 * t
            live = jnp.where(col >= wave, 1.0, 0.0).astype(F32)
            h = h_ref[t:TILES, :]
            for part in range(2):
                live_ref[pl.ds(at + part, n, stride=2), :] = live
                hp_ref[pl.ds(at + part, n, stride=2), :] = h
            for a, base in enumerate(BASES):
                s_even = base * (1 if par == 0 else -1)
                shift = jnp.where(odd == 1, -s_even, s_even)
                place = jnp.where(odd == 1, PLACE[-s_even], PLACE[s_even])
                low = jnp.where(wave + shift < 0, 2 * WAVES, jnp.maximum(wave, wave + shift))
                c = c_ref[pl.ds((fold * TILES + t) * 4 + place, n, stride=4), :]
                c = jnp.where(col >= low, c, 0.0)
                for part in range(2):
                    ck_ref[a, pl.ds(at + part, n, stride=2), :] = c
        pad = pl.ds(par * HALF + 110, 2)
        zero = jnp.zeros((2, 128), F32)
        live_ref[pad, :] = zero
        hp_ref[pad, :] = zero
        for a in range(4):
            ck_ref[a, pad, :] = zero


def prep(info, c, h):
    rows = jax.ShapeDtypeStruct((2 * HALF, 128), F32)
    vmem = pl.BlockSpec(memory_space=pltpu.VMEM)
    return pl.pallas_call(
        prep_kernel,
        out_shape=(jax.ShapeDtypeStruct((4, 2 * HALF, 128), F32), rows, rows),
        in_specs=[pl.BlockSpec(memory_space=pltpu.SMEM), vmem, vmem],
        out_specs=(vmem, vmem, vmem),
        name="prep",
    )(info, c, h)


def mix_kernel(info, w_ref, d_ref, h_ref, x_ref, o_ref):
    w = w_ref[...].astype(jnp.bfloat16)
    d = d_ref[...]
    x2 = x_ref.reshape(LEV * 8, 128)
    o2 = o_ref.reshape(LEV * 8, 128)
    for r in range(0, 8, 2):
        h = h_ref[0, r : r + 1, :]
        scale = 1.0 / (1.0 + h * d)
        highs, lows = [], []
        for e in range(2):
            f = x2[pl.ds(r + e, LEV, stride=8), :] * scale
            high = f.astype(jnp.bfloat16).astype(F32)
            highs.append(high)
            lows.append(f - high)
        high = jnp.concatenate(highs, axis=1)
        low = jnp.concatenate(lows, axis=1)
        both = jnp.concatenate([high, high, low], axis=0).astype(jnp.bfloat16)
        out = jnp.dot(w, both, preferred_element_type=F32)
        for e in range(2):
            o2[pl.ds(r + e, LEV, stride=8), :] = out[:, e * 128 : (e + 1) * 128] * h


def mix(info, w3, diag, hp, x):
    return pl.pallas_call(
        mix_kernel,
        out_shape=jax.ShapeDtypeStruct((LEV, QROWS, 128), F32),
        grid_spec=pltpu.PrefetchScalarGridSpec(
            num_scalar_prefetch=1,
            grid=(QROWS // 8,),
            in_specs=[
                pl.BlockSpec((LEV, 3 * LEV), lambda i, s: (0, 0)),
                pl.BlockSpec((LEV, 1), lambda i, s: (0, 0)),
                pl.BlockSpec((1, 8, 128), lambda i, s: (s[2], i, 0)),
                pl.BlockSpec((LEV, 8, 128), lambda i, s: (0, i, 0)),
            ],
            out_specs=pl.BlockSpec((LEV, 8, 128), lambda i, s: (0, i, 0)),
        ),
        name="mix",
    )(info, w3, diag, hp, x)


def fold_sum(acc, slot, value):
    acc[slot] += jnp.sum((value * value).reshape(QROWS // 8, 8, 128), axis=0)


def near_kernel(info, d_ref, ck_ref, hp_ref, live_ref, p_ref, q_ref, x_ref, y_ref, z_ref, o_ref, s_ref, fix):
    tl = STEP
    step = pl.program_id(0)
    received = (x_ref, y_ref, z_ref)

    @pl.when(step == 0)
    def _():
        s_ref[...] = jnp.zeros_like(s_ref)
        fix[...] = jnp.zeros_like(fix)

    def one(l, get):
        d = d_ref[info[2] * OWN + step * tl + l]
        for q in range(4):
            live = live_ref[q]
            v = p_ref[q, l] * live
            scale = 1.0 / (1.0 + hp_ref[q] * d)
            near = ck_ref[0, q] * q_ref[q, l] + v
            for a in range(3):
                near = near + ck_ref[a + 1, q] * get(a, q)
            o_ref[q, l] = v - scale * near * live
            fold_sum(s_ref, 0, v)

    @pl.when(info[0] > 1)
    def _():
        def level(l, _):
            one(l, lambda a, q: received[a][jnp.where(info[3 + a] == 1, q ^ 2, q), l])
            return 0

        lax.fori_loop(0, tl, level, 0)

    @pl.when(info[0] <= 1)
    def _():
        def level(l, _):
            for a in range(3):

                @pl.when(info[3 + a] == 2)
                def _():
                    for s, t, n in DOWN:
                        fix[a, t // QROWS, t % QROWS : t % QROWS + n, :] = received[a][s // QROWS, l, s % QROWS : s % QROWS + n, :]

                @pl.when(info[3 + a] != 2)
                def _():
                    fix[a] = received[a][:, l]

            one(l, lambda a, q: fix[a, q])
            return 0

        lax.fori_loop(0, tl, level, 0)


def whole(shape):
    return pl.BlockSpec(shape, lambda i, s: (0,) * len(shape))


BLOCK = pl.BlockSpec((4, STEP, QROWS, 128), lambda i, s: (0, i, 0, 0))
SMEM = pl.BlockSpec(memory_space=pltpu.SMEM)
SUM = jax.ShapeDtypeStruct((1, 8, 128), F32)


def near(info, diag, ck, hp, live, p, q, x, y, z):
    return pl.pallas_call(
        near_kernel,
        out_shape=(jax.ShapeDtypeStruct(p.shape, F32), SUM),
        grid_spec=pltpu.PrefetchScalarGridSpec(
            num_scalar_prefetch=1,
            grid=(OWN // STEP,),
            in_specs=[SMEM, whole((4, 4, QROWS, 128)), whole((4, QROWS, 128)), whole((4, QROWS, 128))] + [BLOCK] * 5,
            out_specs=[BLOCK, whole((1, 8, 128))],
            scratch_shapes=[pltpu.VMEM((3, 4, QROWS, 128), F32)],
        ),
        name="near",
    )(info, diag, ck, hp, live, p, q, x, y, z)


def finish_kernel(info, d_ref, hp_ref, live_ref, p_ref, part_ref, m_ref, o_ref, buf):
    step = pl.program_id(0)
    for l in range(STEP):
        d = d_ref[info[2] * OWN + step * STEP + l]
        for q in range(4):
            live = live_ref[q]
            scale = 1.0 / (1.0 + hp_ref[q] * d)
            residual = part_ref[q, l] - m_ref[q, l] * live
            buf[l, q * QROWS : (q + 1) * QROWS, :] = scale * (p_ref[q, l] * live + residual)
    for t in range(1, TILES):
        for par in range(2):
            o_ref[:, 2 * t + par, :, : 128 * t] = jnp.zeros((STEP, 2, 128 * t), F32)
    for fold, j, row in LIVE:
        o_ref[:, fold, :, 128 * j : 128 * j + 128] = buf[:, row : row + 2, :]


def finish(info, diag, hp, live, p, part, m):
    return pl.pallas_call(
        finish_kernel,
        out_shape=jax.ShapeDtypeStruct((OWN, FOLDS, 2, WAVES), F32),
        grid_spec=pltpu.PrefetchScalarGridSpec(
            num_scalar_prefetch=1,
            grid=(OWN // STEP,),
            in_specs=[SMEM, whole((4, QROWS, 128)), whole((4, QROWS, 128))] + [BLOCK] * 3,
            out_specs=pl.BlockSpec((STEP, FOLDS, 2, WAVES), lambda i, s: (i, 0, 0, 0)),
            scratch_shapes=[pltpu.VMEM((STEP, 2 * HALF, 128), F32)],
        ),
        name="finish",
    )(info, diag, hp, live, p, part, m)


def squares_kernel(v_ref, live_ref, part_ref, m_ref, o_ref, acc):
    step = pl.program_id(0)

    @pl.when(step == 0)
    def _():
        acc[...] = jnp.zeros_like(acc)

    for l in range(SQUARES_STEP):
        for q in range(4):
            fold_sum(acc, 0, part_ref[q, l] - m_ref[q, l] * live_ref[q])

    @pl.when(step == pl.num_programs(0) - 1)
    def _():
        row = lax.broadcasted_iota(jnp.int32, (8, 128), 0)
        o_ref[...] = jnp.where(row == 0, jnp.sum(v_ref[0]), jnp.sum(acc[0]))


SQUARES_STEP = 6


def squares(v_sum, live, part, m):
    full = lambda shape: pl.BlockSpec(shape, lambda i: (0,) * len(shape))
    block = pl.BlockSpec((4, SQUARES_STEP, QROWS, 128), lambda i: (0, i, 0, 0))
    return pl.pallas_call(
        squares_kernel,
        out_shape=jax.ShapeDtypeStruct((8, 128), F32),
        grid=(OWN // SQUARES_STEP,),
        in_specs=[full((1, 8, 128)), full((4, QROWS, 128)), block, block],
        out_specs=full((8, 128)),
        scratch_shapes=[pltpu.VMEM((1, 8, 128), F32)],
        name="squares",
    )(v_sum, live, part, m)


def routes(owners):
    x, y = [], []
    for o in range(owners):
        down = o - 2 if o >= 2 else 1 - o
        up = o + 2 if o + 2 < owners else 2 * owners - 1 - (o + 2)
        x.append((o, down if o % 2 == 0 else up))
        y.append((o, up if o % 2 == 0 else down))
    return x, y, [(o, o ^ 1) for o in range(owners)]


def total(value, axes):
    n = lax.axis_size(axes)
    every = lax.all_to_all(jnp.broadcast_to(value[None], (n,) + value.shape), axes, 0, 0, tiled=True)
    return jnp.sum(every, axis=0)


def body(forcing, coupling, helmholtz, vertical):
    owner = lax.axis_index(MA).astype(jnp.int32)
    lev = lax.axis_index("lev").astype(jnp.int32)
    ends = {"x": (1, OWNERS - 2), "y": (0, OWNERS - 1), "z": (0, OWNERS - 1)}
    modes = [jnp.where(owner == low, 2, jnp.where(owner == high, 1, 0)) for low, high in ends.values()]
    info = jnp.stack([owner, owner & 1, lev] + modes).astype(jnp.int32)
    crows = coupling.reshape(4, FOLDS, TILES, 128).transpose(1, 2, 0, 3).reshape(800, 128)
    p = pack(forcing.transpose(0, 2, 1, 3))
    to_x, to_y, swap = routes(OWNERS)
    every = lax.all_to_all(p, "lev", 0, 0, tiled=True).reshape(LEV, QROWS, 128)
    x = lax.ppermute(p, MA, to_x)
    q = lax.ppermute(p, MA, swap)
    x, p_after = lax.optimization_barrier((x, p))
    y = lax.ppermute(p_after, MA, to_y)
    z = lax.ppermute(x, MA, swap)
    ck, hp, live = prep(info, crows, helmholtz.reshape(TILES, 128))
    ck = ck.reshape(4, 4, QROWS, 128)
    hp = hp.reshape(4, QROWS, 128)
    live = live.reshape(4, QROWS, 128)
    diag = jnp.sum(vertical * jnp.eye(LEV, dtype=F32), axis=1)
    high = lax.reduce_precision(vertical, 8, 7)
    w3 = jnp.concatenate([high, vertical - high, high], axis=1)
    m = mix(info, w3, diag[:, None], hp, every).reshape(4, OWN, QROWS, 128)
    m = lax.all_to_all(m, "lev", 0, 0, tiled=True)
    part, v_sum = near(info, diag, ck, hp, live, p, q, x, y, z)
    part, m = lax.optimization_barrier((part, m))
    sums = total(squares(v_sum, live, part, m), ("ma_1", "ma_2"))
    rows = finish(info, diag, hp, live, p, part, m)
    sums, rows = lax.optimization_barrier((sums, rows))
    sums = total(sums, ("ma_0", "lev"))
    norms = jnp.sqrt(sums[:2, 0] / (LEV * WAVES * (WAVES + 1)))
    return (rows.transpose(0, 2, 1, 3), norms)


def solution(mesh):
    split = Mesh(mesh.devices.reshape(4, 8, 2, mesh.shape["lev"]), ("ma_0", "ma_1", "ma_2", "lev"))
    return jax.shard_map(
        body,
        mesh=split,
        in_specs=(P("lev", None, MA, None), P(None, MA, None), P(), P()),
        out_specs=(P("lev", None, MA, None), P()),
        check_vma=False,
    )
```

```python
import jax
import jax.numpy as jnp
from jax import lax
from jax.experimental import pallas as pl
from jax.experimental.pallas import tpu as pltpu
from jax.sharding import Mesh
from jax.sharding import PartitionSpec as P

LEV = 72
WAVES = 1280
OWNERS = 64
FOLDS = 20
TILES = 10
HALF = 112
QROWS = 56
OWN = 18
STEP = 9
MA = ("ma_0", "ma_1", "ma_2")
F32 = jnp.float32


def start_row(t):
    return 20 * t - t * (t - 1)


def cut(moves):
    out = []
    for s, d, n in moves:
        while n:
            step = min(n, QROWS - d % QROWS, QROWS - s % QROWS)
            out.append((s, d, step))
            s, d, n = s + step, d + step, n - step
    return out


LIVE = [
    (2 * t + par, j, par * HALF + start_row(t) + 2 * (j - t)) for par in range(2) for t in range(TILES) for j in range(t, TILES)
]
DOWN = cut(
    [(start_row(t + 1), HALF + start_row(t) + 2, 18 - 2 * t) for t in range(TILES - 1)]
    + [(HALF + start_row(t - 1) + 2, start_row(t), 20 - 2 * t) for t in range(1, TILES)]
)


def pack_kernel(x_ref, p_ref):
    for fold, j, row in LIVE:
        q, r = divmod(row, QROWS)
        p_ref[q, :, r : r + 2, :] = x_ref[:, fold, :, 128 * j : 128 * j + 128]
    for q in (1, 3):
        p_ref[q, :, QROWS - 2 :, :] = jnp.zeros((p_ref.shape[1], 2, 128), F32)


def pack(x):
    return pl.pallas_call(
        pack_kernel,
        out_shape=jax.ShapeDtypeStruct((4, OWN, QROWS, 128), F32),
        grid=(OWN // STEP,),
        in_specs=[pl.BlockSpec((STEP, FOLDS, 2, WAVES), lambda i: (i, 0, 0, 0))],
        out_specs=pl.BlockSpec((4, STEP, QROWS, 128), lambda i: (0, i, 0, 0)),
        name="pack",
    )(x)


BASES = (1, 2, -2, -1)
PLACE = {-2: 0, -1: 1, 1: 2, 2: 3}


def prep_kernel(info, c_ref, h_ref, ck_ref, hp_ref, live_ref):
    owner = info[0]
    odd = info[1]
    for par in range(2):
        for t in range(TILES):
            fold = 2 * t + par
            n = TILES - t
            at = par * HALF + start_row(t)
            wave = fold * OWNERS + (owner if par == 0 else OWNERS - 1 - owner)
            col = lax.broadcasted_iota(jnp.int32, (n, 128), 0) * 128 + lax.broadcasted_iota(jnp.int32, (n, 128), 1) + 128 * t
            live = jnp.where(col >= wave, 1.0, 0.0).astype(F32)
            h = h_ref[t:TILES, :]
            for part in range(2):
                live_ref[pl.ds(at + part, n, stride=2), :] = live
                hp_ref[pl.ds(at + part, n, stride=2), :] = h
            for a, base in enumerate(BASES):
                s_even = base * (1 if par == 0 else -1)
                shift = jnp.where(odd == 1, -s_even, s_even)
                place = jnp.where(odd == 1, PLACE[-s_even], PLACE[s_even])
                low = jnp.where(wave + shift < 0, 2 * WAVES, jnp.maximum(wave, wave + shift))
                c = c_ref[pl.ds((fold * TILES + t) * 4 + place, n, stride=4), :]
                c = jnp.where(col >= low, c, 0.0)
                for part in range(2):
                    ck_ref[a, pl.ds(at + part, n, stride=2), :] = c
        pad = pl.ds(par * HALF + 110, 2)
        zero = jnp.zeros((2, 128), F32)
        live_ref[pad, :] = zero
        hp_ref[pad, :] = zero
        for a in range(4):
            ck_ref[a, pad, :] = zero


def prep(info, c, h):
    rows = jax.ShapeDtypeStruct((2 * HALF, 128), F32)
    vmem = pl.BlockSpec(memory_space=pltpu.VMEM)
    return pl.pallas_call(
        prep_kernel,
        out_shape=(jax.ShapeDtypeStruct((4, 2 * HALF, 128), F32), rows, rows),
        in_specs=[pl.BlockSpec(memory_space=pltpu.SMEM), vmem, vmem],
        out_specs=(vmem, vmem, vmem),
        name="prep",
    )(info, c, h)


def mix_kernel(info, w_ref, d_ref, h_ref, x_ref, o_ref):
    w = w_ref[...].astype(jnp.bfloat16)
    d = d_ref[...]
    x2 = x_ref.reshape(LEV * QROWS, 128)
    o2 = o_ref.reshape(LEV * QROWS, 128)
    for r in range(0, QROWS, 2):
        h = h_ref[0, r : r + 1, :]
        scale = 1.0 / (1.0 + h * d)
        highs, lows = [], []
        for e in range(2):
            f = x2[pl.ds(r + e, LEV, stride=QROWS), :] * scale
            high = f.astype(jnp.bfloat16).astype(F32)
            highs.append(high)
            lows.append(f - high)
        high = jnp.concatenate(highs, axis=1)
        low = jnp.concatenate(lows, axis=1)
        both = jnp.concatenate([high, high, low], axis=0).astype(jnp.bfloat16)
        out = jnp.dot(w, both, preferred_element_type=F32)
        for e in range(2):
            o2[pl.ds(r + e, LEV, stride=QROWS), :] = out[:, e * 128 : (e + 1) * 128] * h


def mix(info, w3, diag, hp, x):
    return pl.pallas_call(
        mix_kernel,
        out_shape=jax.ShapeDtypeStruct((LEV, QROWS, 128), F32),
        grid_spec=pltpu.PrefetchScalarGridSpec(
            num_scalar_prefetch=1,
            grid=(1,),
            in_specs=[
                pl.BlockSpec((LEV, 3 * LEV), lambda i, s: (0, 0)),
                pl.BlockSpec((LEV, 1), lambda i, s: (0, 0)),
                pl.BlockSpec((1, QROWS, 128), lambda i, s: (s[2], 0, 0)),
                pl.BlockSpec((LEV, QROWS, 128), lambda i, s: (0, 0, 0)),
            ],
            out_specs=pl.BlockSpec((LEV, QROWS, 128), lambda i, s: (0, 0, 0)),
        ),
        name="mix",
    )(info, w3, diag, hp, x)


def fold_sum(acc, slot, value):
    acc[slot] += jnp.sum((value * value).reshape(QROWS // 8, 8, 128), axis=0)


def near_kernel(info, d_ref, ck_ref, hp_ref, live_ref, p_ref, q_ref, x_ref, y_ref, z_ref, o_ref, s_ref, fix):
    tl = STEP
    step = pl.program_id(0)
    received = (x_ref, y_ref, z_ref)

    @pl.when(step == 0)
    def _():
        s_ref[...] = jnp.zeros_like(s_ref)
        fix[...] = jnp.zeros_like(fix)

    def one(l, get):
        d = d_ref[info[2] * OWN + step * tl + l]
        for q in range(4):
            live = live_ref[q]
            v = p_ref[q, l] * live
            scale = 1.0 / (1.0 + hp_ref[q] * d)
            near = ck_ref[0, q] * q_ref[q, l] + v
            for a in range(3):
                near = near + ck_ref[a + 1, q] * get(a, q)
            o_ref[q, l] = v - scale * near * live
            fold_sum(s_ref, 0, v)

    @pl.when(info[0] > 1)
    def _():
        def level(l, _):
            one(l, lambda a, q: received[a][jnp.where(info[3 + a] == 1, q ^ 2, q), l])
            return 0

        lax.fori_loop(0, tl, level, 0)

    @pl.when(info[0] <= 1)
    def _():
        def level(l, _):
            for a in range(3):

                @pl.when(info[3 + a] == 2)
                def _():
                    for s, t, n in DOWN:
                        fix[a, t // QROWS, t % QROWS : t % QROWS + n, :] = received[a][s // QROWS, l, s % QROWS : s % QROWS + n, :]

                @pl.when(info[3 + a] != 2)
                def _():
                    fix[a] = received[a][:, l]

            one(l, lambda a, q: fix[a, q])
            return 0

        lax.fori_loop(0, tl, level, 0)


def whole(shape):
    return pl.BlockSpec(shape, lambda i, s: (0,) * len(shape))


BLOCK = pl.BlockSpec((4, STEP, QROWS, 128), lambda i, s: (0, i, 0, 0))
SMEM = pl.BlockSpec(memory_space=pltpu.SMEM)
SUM = jax.ShapeDtypeStruct((1, 8, 128), F32)


def near(info, diag, ck, hp, live, p, q, x, y, z):
    return pl.pallas_call(
        near_kernel,
        out_shape=(jax.ShapeDtypeStruct(p.shape, F32), SUM),
        grid_spec=pltpu.PrefetchScalarGridSpec(
            num_scalar_prefetch=1,
            grid=(OWN // STEP,),
            in_specs=[SMEM, whole((4, 4, QROWS, 128)), whole((4, QROWS, 128)), whole((4, QROWS, 128))] + [BLOCK] * 5,
            out_specs=[BLOCK, whole((1, 8, 128))],
            scratch_shapes=[pltpu.VMEM((3, 4, QROWS, 128), F32)],
        ),
        name="near",
    )(info, diag, ck, hp, live, p, q, x, y, z)


def finish_kernel(base, info, d_ref, hp_ref, live_ref, p_ref, part_ref, m_ref, *refs):
    o_ref, buf = refs[-2:]
    step = base // FINISH_STEP + pl.program_id(0)
    for l in range(FINISH_STEP):
        d = d_ref[info[2] * OWN + step * FINISH_STEP + l]
        for q in range(4):
            live = live_ref[q]
            scale = 1.0 / (1.0 + hp_ref[q] * d)
            residual = part_ref[q, l] - m_ref[q, l] * live
            buf[l, q * QROWS : (q + 1) * QROWS, :] = scale * (p_ref[q, l] * live + residual)
    for t in range(1, TILES):
        for par in range(2):
            o_ref[:, 2 * t + par, :, : 128 * t] = jnp.zeros((FINISH_STEP, 2, 128 * t), F32)
    for fold, j, row in LIVE:
        o_ref[:, fold, :, 128 * j : 128 * j + 128] = buf[:, row : row + 2, :]


def finish(base, info, diag, hp, live, p, part, m, rows=None):
    at = base // FINISH_STEP
    block = pl.BlockSpec((4, FINISH_STEP, QROWS, 128), lambda i, s: (0, i + at, 0, 0))
    before = [] if rows is None else [rows]
    return pl.pallas_call(
        lambda *refs: finish_kernel(base, *refs),
        out_shape=jax.ShapeDtypeStruct((OWN, FOLDS, 2, WAVES), F32),
        grid_spec=pltpu.PrefetchScalarGridSpec(
            num_scalar_prefetch=1,
            grid=(OWN // 2 // FINISH_STEP,),
            in_specs=[SMEM, whole((4, QROWS, 128)), whole((4, QROWS, 128))]
            + [block] * 3
            + [pl.BlockSpec(memory_space=pl.ANY)] * len(before),
            out_specs=pl.BlockSpec((FINISH_STEP, FOLDS, 2, WAVES), lambda i, s: (i + at, 0, 0, 0)),
            scratch_shapes=[pltpu.VMEM((FINISH_STEP, 2 * HALF, 128), F32)],
        ),
        input_output_aliases={7: 0} if before else {},
        name="finish",
    )(info, diag, hp, live, p, part, m, *before)


def squares_kernel(v_ref, live_ref, part_ref, m_ref, o_ref, acc):
    step = pl.program_id(0)

    @pl.when(step == 0)
    def _():
        acc[...] = jnp.zeros_like(acc)

    for l in range(SQUARES_STEP):
        for q in range(4):
            fold_sum(acc, 0, part_ref[q, l] - m_ref[q, l] * live_ref[q])

    @pl.when(step == pl.num_programs(0) - 1)
    def _():
        row = lax.broadcasted_iota(jnp.int32, (8, 128), 0)
        both = jnp.where(row == 0, jnp.sum(v_ref[0]), jnp.sum(acc[0]))
        o_ref[...] = jnp.broadcast_to(both, o_ref.shape)


SQUARES_STEP = 9
FINISH_STEP = 9


def squares(copies, v_sum, live, part, m):
    full = lambda shape: pl.BlockSpec(shape, lambda i: (0,) * len(shape))
    block = pl.BlockSpec((4, SQUARES_STEP, QROWS, 128), lambda i: (0, i, 0, 0))
    return pl.pallas_call(
        squares_kernel,
        out_shape=jax.ShapeDtypeStruct((copies, 8, 128), F32),
        grid=(OWN // SQUARES_STEP,),
        in_specs=[full((1, 8, 128)), full((4, QROWS, 128)), block, block],
        out_specs=full((copies, 8, 128)),
        scratch_shapes=[pltpu.VMEM((1, 8, 128), F32)],
        name="squares",
    )(v_sum, live, part, m)


def routes(owners):
    x, y = [], []
    for o in range(owners):
        down = o - 2 if o >= 2 else 1 - o
        up = o + 2 if o + 2 < owners else 2 * owners - 1 - (o + 2)
        x.append((o, down if o % 2 == 0 else up))
        y.append((o, up if o % 2 == 0 else down))
    return x, y, [(o, o ^ 1) for o in range(owners)]


def total(copies, axes):
    return jnp.sum(lax.all_to_all(copies, axes, 0, 0, tiled=True), axis=0)


def body(forcing, coupling, helmholtz, vertical):
    owner = lax.axis_index(MA).astype(jnp.int32)
    lev = lax.axis_index("lev").astype(jnp.int32)
    ends = {"x": (1, OWNERS - 2), "y": (0, OWNERS - 1), "z": (0, OWNERS - 1)}
    modes = [jnp.where(owner == low, 2, jnp.where(owner == high, 1, 0)) for low, high in ends.values()]
    info = jnp.stack([owner, owner & 1, lev] + modes).astype(jnp.int32)
    crows = coupling.reshape(4, FOLDS, TILES, 128).transpose(1, 2, 0, 3).reshape(800, 128)
    p = pack(forcing.transpose(0, 2, 1, 3))
    to_x, to_y, swap = routes(OWNERS)
    every = lax.all_to_all(p, "lev", 0, 0, tiled=True).reshape(LEV, QROWS, 128)
    x = lax.ppermute(p, MA, to_x)
    q = lax.ppermute(p, MA, swap)
    ck, hp, live = prep(info, crows, helmholtz.reshape(TILES, 128))
    diag = jnp.sum(vertical * jnp.eye(LEV, dtype=F32), axis=1)
    column = diag[:, None]
    high = lax.reduce_precision(vertical, 8, 7)
    w3 = jnp.concatenate([high, vertical - high, high], axis=1)
    x, p_after, ck, hp, live, w3, column = lax.optimization_barrier((x, p, ck, hp, live, w3, column))
    y = lax.ppermute(p_after, MA, to_y)
    z = lax.ppermute(x, MA, swap)
    ck = ck.reshape(4, 4, QROWS, 128)
    hp = hp.reshape(4, QROWS, 128)
    live = live.reshape(4, QROWS, 128)
    m = mix(info, w3, column, hp, every).reshape(4, OWN, QROWS, 128)
    m = lax.all_to_all(m, "lev", 0, 0, tiled=True)
    part, v_sum = near(info, diag, ck, hp, live, p, q, x, y, z)
    part, m = lax.optimization_barrier((part, m))
    inner, outer = ("ma_1", "ma_2"), ("ma_0", "lev")
    sums = total(squares(lax.axis_size(inner), v_sum, live, part, m), inner)
    rows = finish(0, info, diag, hp, live, p, part, m)
    sums, rows = lax.optimization_barrier((sums, rows))
    sums = total(jnp.broadcast_to(sums[None], (lax.axis_size(outer), 8, 128)), outer)
    rows = finish(OWN // 2, info, diag, hp, live, p, part, m, rows)
    norms = jnp.sqrt(sums[:2, 0] / (LEV * WAVES * (WAVES + 1)))
    return (rows.transpose(0, 2, 1, 3), norms)


def solution(mesh):
    split = Mesh(mesh.devices.reshape(4, 8, 2, mesh.shape["lev"]), ("ma_0", "ma_1", "ma_2", "lev"))
    return jax.shard_map(
        body,
        mesh=split,
        in_specs=(P("lev", None, MA, None), P(None, MA, None), P(), P()),
        out_specs=(P("lev", None, MA, None), P()),
        check_vma=False,
    )
```

```python
import jax
import jax.numpy as jnp
from jax import lax
from jax.experimental import pallas as pl
from jax.experimental.pallas import tpu as pltpu
from jax.sharding import Mesh
from jax.sharding import PartitionSpec as P

LEV = 72
WAVES = 1280
OWNERS = 64
FOLDS = 20
TILES = 10
HALF = 112
QROWS = 56
OWN = 18
STEP = 9
MA = ("ma_0", "ma_1", "ma_2")
F32 = jnp.float32
VMEM = pl.BlockSpec(memory_space=pltpu.VMEM)
SMEM = pl.BlockSpec(memory_space=pltpu.SMEM)
QUARTER = jax.ShapeDtypeStruct((OWN, QROWS, 128), F32)


def in_vmem(x):
    return pltpu.with_memory_space_constraint(x, pltpu.VMEM)


def start_row(t):
    return 20 * t - t * (t - 1)


def cut(moves):
    out = []
    for s, d, n in moves:
        while n:
            step = min(n, QROWS - d % QROWS, QROWS - s % QROWS)
            out.append((s, d, step))
            s, d, n = s + step, d + step, n - step
    return out


LIVE = [
    (2 * t + par, j, par * HALF + start_row(t) + 2 * (j - t)) for par in range(2) for t in range(TILES) for j in range(t, TILES)
]
DOWN = cut(
    [(start_row(t + 1), HALF + start_row(t) + 2, 18 - 2 * t) for t in range(TILES - 1)]
    + [(HALF + start_row(t - 1) + 2, start_row(t), 20 - 2 * t) for t in range(1, TILES)]
)


def pack_kernel(x_ref, p_ref):
    for fold, j, row in LIVE:
        q, r = divmod(row, QROWS)
        p_ref[q, :, r : r + 2, :] = x_ref[:, fold, :, 128 * j : 128 * j + 128]
    for q in (1, 3):
        p_ref[q, :, QROWS - 2 :, :] = jnp.zeros((p_ref.shape[1], 2, 128), F32)


def pack(x):
    return pl.pallas_call(
        pack_kernel,
        out_shape=jax.ShapeDtypeStruct((4, OWN, QROWS, 128), F32),
        grid=(OWN // STEP,),
        in_specs=[pl.BlockSpec((STEP, FOLDS, 2, WAVES), lambda i: (i, 0, 0, 0))],
        out_specs=pl.BlockSpec((4, STEP, QROWS, 128), lambda i: (0, i, 0, 0)),
        name="pack",
    )(x)


BASES = (1, 2, -2, -1)
PLACE = {-2: 0, -1: 1, 1: 2, 2: 3}


def prep_kernel(info, c_ref, h_ref, ck_ref, hp_ref, live_ref):
    owner = info[0]
    odd = info[1]
    for par in range(2):
        for t in range(TILES):
            fold = 2 * t + par
            n = TILES - t
            at = par * HALF + start_row(t)
            wave = fold * OWNERS + (owner if par == 0 else OWNERS - 1 - owner)
            col = lax.broadcasted_iota(jnp.int32, (n, 128), 0) * 128 + lax.broadcasted_iota(jnp.int32, (n, 128), 1) + 128 * t
            live = jnp.where(col >= wave, 1.0, 0.0).astype(F32)
            h = h_ref[t:TILES, :]
            for part in range(2):
                live_ref[pl.ds(at + part, n, stride=2), :] = live
                hp_ref[pl.ds(at + part, n, stride=2), :] = h
            for a, base in enumerate(BASES):
                s_even = base * (1 if par == 0 else -1)
                shift = jnp.where(odd == 1, -s_even, s_even)
                place = jnp.where(odd == 1, PLACE[-s_even], PLACE[s_even])
                low = jnp.where(wave + shift < 0, 2 * WAVES, jnp.maximum(wave, wave + shift))
                c = c_ref[pl.ds((fold * TILES + t) * 4 + place, n, stride=4), :]
                c = jnp.where(col >= low, c, 0.0)
                for part in range(2):
                    ck_ref[a, pl.ds(at + part, n, stride=2), :] = c
        pad = pl.ds(par * HALF + 110, 2)
        zero = jnp.zeros((2, 128), F32)
        live_ref[pad, :] = zero
        hp_ref[pad, :] = zero
        for a in range(4):
            ck_ref[a, pad, :] = zero


def prep(info, c, h):
    rows = jax.ShapeDtypeStruct((2 * HALF, 128), F32)
    vmem = pl.BlockSpec(memory_space=pltpu.VMEM)
    return pl.pallas_call(
        prep_kernel,
        out_shape=(jax.ShapeDtypeStruct((4, 2 * HALF, 128), F32), rows, rows),
        in_specs=[pl.BlockSpec(memory_space=pltpu.SMEM), vmem, vmem],
        out_specs=(vmem, vmem, vmem),
        name="prep",
    )(info, c, h)


ROWS = 24


def mix_kernel(info, w_ref, h_ref, *refs):
    x_ref, *outs = refs
    w = w_ref[:, : 3 * LEV].astype(jnp.bfloat16)
    d = w_ref[:LEV, 3 * LEV :]
    x2 = x_ref.reshape(LEV * QROWS, 128)
    for r in range(0, QROWS, 2):
        h = h_ref[0, r : r + 1, :]
        scale = 1.0 / (1.0 + h * d)
        highs, lows = [], []
        for e in range(2):
            f = x2[pl.ds(r + e, LEV, stride=QROWS), :] * scale
            high = f.astype(jnp.bfloat16).astype(F32)
            highs.append(high)
            lows.append(f - high)
        high = jnp.concatenate(highs, axis=1)
        low = jnp.concatenate(lows, axis=1)
        both = jnp.concatenate([high, high, low], axis=0).astype(jnp.bfloat16)
        out = jnp.dot(w, both, preferred_element_type=F32)
        for away, ref in enumerate(outs):
            o2 = ref.reshape(OWN * QROWS, 128)
            for e in range(2):
                part = out[away * ROWS : away * ROWS + OWN, e * 128 : (e + 1) * 128]
                o2[pl.ds(r + e, OWN, stride=QROWS), :] = part * h


def mix(info, w3, hp, x):
    held = pl.BlockSpec((OWN, QROWS, 128), lambda i, s: (0, 0, 0))
    return pl.pallas_call(
        mix_kernel,
        out_shape=[QUARTER] * 4,
        grid_spec=pltpu.PrefetchScalarGridSpec(
            num_scalar_prefetch=1,
            grid=(1,),
            in_specs=[
                pl.BlockSpec((4 * ROWS, 3 * LEV + 1), lambda i, s: (0, 0)),
                pl.BlockSpec((1, QROWS, 128), lambda i, s: (s[2], 0, 0)),
                VMEM,
            ],
            out_specs=[held] * 4,
        ),
        name="mix",
    )(info, w3, hp, in_vmem(x))


def mix_table(vertical, lev):
    diag = jnp.sum(vertical * jnp.eye(LEV, dtype=F32), axis=1)
    padded = jnp.pad(vertical.reshape(4, OWN, LEV), ((0, 0), (0, ROWS - OWN), (0, 0))).reshape(4 * ROWS, LEV)
    turned = lax.dynamic_slice_in_dim(jnp.concatenate([padded, padded], axis=0), lev * ROWS, 4 * ROWS, 0)
    high = lax.reduce_precision(turned, 8, 7)
    column = jnp.pad(diag[:, None], ((0, 4 * ROWS - LEV), (0, 0)))
    return diag, jnp.concatenate([high, turned - high, high, column], axis=1)


def fold_sum(acc, slot, value):
    acc[slot] += jnp.sum((value * value).reshape(QROWS // 8, 8, 128), axis=0)


def near_kernel(info, d_ref, ck_ref, hp_ref, live_ref, p_ref, q_ref, x_ref, y_ref, z_ref, o_ref, kept_ref, s_ref, fix):
    step = pl.program_id(0)
    received = (x_ref, y_ref, z_ref)

    @pl.when(step == 0)
    def _():
        s_ref[...] = jnp.zeros_like(s_ref)

    def every(get):
        def chunk(c, _):
            rows = pl.ds(pl.multiple_of(c * 8, 8), 8)
            for q in range(4):
                live, hp = live_ref[q, rows, :], hp_ref[q, rows, :]
                ck = [ck_ref[a, q, rows, :] for a in range(4)]
                squares = jnp.zeros((8, 128), F32)
                for l in range(STEP):
                    scale = 1.0 / (1.0 + hp * d_ref[info[2] * OWN + step * STEP + l])
                    v = p_ref[q, l, rows, :] * live
                    near = ck[0] * q_ref[q, l, rows, :] + v
                    for a in range(3):
                        near = near + ck[a + 1] * get(a, q, l, rows)
                    left = v - scale * near * live
                    o_ref[q, l, rows, :] = left
                    kept_ref[q, step * STEP + l, rows, :] = left
                    squares = squares + v * v
                s_ref[0] += squares
            return 0

        lax.fori_loop(0, QROWS // 8, chunk, 0)

    @pl.when(info[0] > 1)
    def _():
        every(lambda a, q, l, rows: received[a][jnp.where(info[3 + a] == 1, q ^ 2, q), l, rows, :])

    @pl.when(info[0] <= 1)
    def _():
        for a in range(3):

            @pl.when(info[3 + a] == 2)
            def _():
                fix[a] = jnp.zeros(fix.shape[1:], F32)
                for s, t, n in DOWN:
                    fix[a, t // QROWS, :, t % QROWS : t % QROWS + n, :] = received[a][s // QROWS, :, s % QROWS : s % QROWS + n, :]

            @pl.when(info[3 + a] != 2)
            def _():
                fix[a] = received[a][...]

        every(lambda a, q, l, rows: fix[a, q, l, rows, :])


def whole(shape):
    return pl.BlockSpec(shape, lambda i, s: (0,) * len(shape))


BLOCK = pl.BlockSpec((4, STEP, QROWS, 128), lambda i, s: (0, i, 0, 0))
SUM = jax.ShapeDtypeStruct((1, 8, 128), F32)


def near(info, diag, ck, hp, live, p, q, x, y, z):
    return pl.pallas_call(
        near_kernel,
        out_shape=(jax.ShapeDtypeStruct(p.shape, F32), pltpu.VMEM(p.shape, F32), SUM),
        grid_spec=pltpu.PrefetchScalarGridSpec(
            num_scalar_prefetch=1,
            grid=(OWN // STEP,),
            in_specs=[SMEM, whole((4, 4, QROWS, 128)), whole((4, QROWS, 128)), whole((4, QROWS, 128))] + [BLOCK] * 5,
            out_specs=[BLOCK, VMEM, whole((1, 8, 128))],
            scratch_shapes=[pltpu.VMEM((3, 4, STEP, QROWS, 128), F32)],
        ),
        name="near",
    )(info, diag, ck, hp, live, p, q, x, y, z)


def finish_kernel(base, info, d_ref, hp_ref, live_ref, p_ref, part_ref, *refs):
    o_ref, buf = refs[-2:]
    step = base // FINISH_STEP + pl.program_id(0)
    for l in range(FINISH_STEP):
        d = d_ref[info[2] * OWN + step * FINISH_STEP + l]
        for away in range(4):
            q = (info[2] - away) & 3
            live = live_ref[q]
            scale = 1.0 / (1.0 + hp_ref[q] * d)
            residual = part_ref[q, l] - refs[away][l] * live
            buf[l, pl.ds(pl.multiple_of(q * QROWS, 8), QROWS), :] = scale * (p_ref[q, l] * live + residual)
    for t in range(1, TILES):
        for par in range(2):
            o_ref[:, 2 * t + par, :, : 128 * t] = jnp.zeros((FINISH_STEP, 2, 128 * t), F32)
    for fold, j, row in LIVE:
        o_ref[:, fold, :, 128 * j : 128 * j + 128] = buf[:, row : row + 2, :]


def finish(base, info, diag, hp, live, p, part, m, *before):
    at = base // FINISH_STEP
    block = pl.BlockSpec((4, FINISH_STEP, QROWS, 128), lambda i, s: (0, i + at, 0, 0))
    piece = pl.BlockSpec((FINISH_STEP, QROWS, 128), lambda i, s: (i + at, 0, 0))
    return pl.pallas_call(
        lambda *refs: finish_kernel(base, *refs),
        out_shape=jax.ShapeDtypeStruct((OWN, FOLDS, 2, WAVES), F32),
        grid_spec=pltpu.PrefetchScalarGridSpec(
            num_scalar_prefetch=1,
            grid=(OWN // 2 // FINISH_STEP,),
            in_specs=[SMEM, whole((4, QROWS, 128)), whole((4, QROWS, 128))]
            + [block] * 2
            + [piece] * 4
            + [pl.BlockSpec(memory_space=pl.ANY)] * len(before),
            out_specs=pl.BlockSpec((FINISH_STEP, FOLDS, 2, WAVES), lambda i, s: (i + at, 0, 0, 0)),
            scratch_shapes=[pltpu.VMEM((FINISH_STEP, 2 * HALF, 128), F32)],
        ),
        input_output_aliases={10: 0} if before else {},
        name="finish",
    )(info, diag, hp, live, p, part, *m, *before)


def squares_kernel(info, v_ref, live_ref, part_ref, *refs):
    o_ref, acc = refs[-2:]
    step = pl.program_id(0)

    @pl.when(step == 0)
    def _():
        acc[...] = jnp.zeros_like(acc)

    def chunk(c, _):
        rows = pl.ds(pl.multiple_of(c * 8, 8), 8)
        sums = [jnp.zeros((8, 128), F32) for _ in range(8)]
        for away in range(4):
            q = (info[2] - away) & 3
            live = live_ref[q, rows, :]
            for l in range(SQUARES_STEP):
                residual = part_ref[q, step * SQUARES_STEP + l, rows, :] - refs[away][l, rows, :] * live
                sums[2 * away + l % 2] += residual * residual
        while len(sums) > 1:
            sums = [a + b for a, b in zip(sums[::2], sums[1::2])]
        acc[0] += sums[0]
        return 0

    lax.fori_loop(0, QROWS // 8, chunk, 0)

    @pl.when(step == pl.num_programs(0) - 1)
    def _():
        row = lax.broadcasted_iota(jnp.int32, (8, 128), 0)
        both = jnp.where(row == 0, jnp.sum(v_ref[0]), jnp.sum(acc[0]))
        o_ref[...] = jnp.broadcast_to(both, o_ref.shape)


SQUARES_STEP = 9
FINISH_STEP = 9


def squares(copies, info, v_sum, live, part, m):
    piece = pl.BlockSpec((SQUARES_STEP, QROWS, 128), lambda i, s: (i, 0, 0))
    return pl.pallas_call(
        squares_kernel,
        out_shape=jax.ShapeDtypeStruct((copies, 8, 128), F32),
        grid_spec=pltpu.PrefetchScalarGridSpec(
            num_scalar_prefetch=1,
            grid=(OWN // SQUARES_STEP,),
            in_specs=[whole((1, 8, 128)), whole((4, QROWS, 128)), VMEM] + [piece] * 4,
            out_specs=whole((copies, 8, 128)),
            scratch_shapes=[pltpu.VMEM((1, 8, 128), F32)],
        ),
        name="squares",
    )(info, v_sum, live, in_vmem(part), *m)


def routes(owners):
    x, y = [], []
    for o in range(owners):
        down = o - 2 if o >= 2 else 1 - o
        up = o + 2 if o + 2 < owners else 2 * owners - 1 - (o + 2)
        x.append((o, down if o % 2 == 0 else up))
        y.append((o, up if o % 2 == 0 else down))
    return x, y, [(o, o ^ 1) for o in range(owners)]


def total(copies, axes):
    return jnp.sum(lax.all_to_all(copies, axes, 0, 0, tiled=True), axis=0)


def body(forcing, coupling, helmholtz, vertical):
    owner = lax.axis_index(MA).astype(jnp.int32)
    lev = lax.axis_index("lev").astype(jnp.int32)
    ends = {"x": (1, OWNERS - 2), "y": (0, OWNERS - 1), "z": (0, OWNERS - 1)}
    modes = [jnp.where(owner == low, 2, jnp.where(owner == high, 1, 0)) for low, high in ends.values()]
    info = jnp.stack([owner, owner & 1, lev] + modes).astype(jnp.int32)
    crows = coupling.reshape(4, FOLDS, TILES, 128).transpose(1, 2, 0, 3).reshape(800, 128)
    p = pack(forcing.transpose(0, 2, 1, 3))
    to_x, to_y, swap = routes(OWNERS)
    along = lambda v, away: lax.ppermute(v, "lev", [(i, (i + away) % 4) for i in range(4)])
    every = lax.all_to_all(p, "lev", 0, 0, tiled=True).reshape(LEV, QROWS, 128)
    x = lax.ppermute(p, MA, to_x)
    q = lax.ppermute(p, MA, swap)
    ck, hp, live = prep(info, crows, helmholtz.reshape(TILES, 128))
    diag, w3 = mix_table(vertical, lev)
    x, p_after, ck, hp, live, w3 = lax.optimization_barrier((x, p, ck, hp, live, w3))
    y = lax.ppermute(p_after, MA, to_y)
    z = lax.ppermute(x, MA, swap)
    ck = ck.reshape(4, 4, QROWS, 128)
    hp = hp.reshape(4, QROWS, 128)
    live = live.reshape(4, QROWS, 128)
    mixed = mix(info, w3, hp, every)
    m = [mixed[0]] + [along(v, away) for v, away in zip(mixed[1:], (1, 2, 3))]
    part, kept, v_sum = near(info, diag, ck, hp, live, p, q, x, y, z)
    part, *m = lax.optimization_barrier((part, *m))
    inner, outer = ("ma_1", "ma_2"), ("ma_0", "lev")
    sums = total(squares(lax.axis_size(inner), info, v_sum, live, kept, m), inner)
    rows = finish(0, info, diag, hp, live, p, part, m)
    sums, rows = lax.optimization_barrier((sums, rows))
    sums = total(jnp.broadcast_to(sums[None], (lax.axis_size(outer), 8, 128)), outer)
    rows = finish(OWN // 2, info, diag, hp, live, p, part, m, rows)
    norms = jnp.sqrt(sums[:2, 0] / (LEV * WAVES * (WAVES + 1)))
    return (rows.transpose(0, 2, 1, 3), norms)


def solution(mesh):
    split = Mesh(mesh.devices.reshape(4, 8, 2, mesh.shape["lev"]), ("ma_0", "ma_1", "ma_2", "lev"))
    return jax.shard_map(
        body,
        mesh=split,
        in_specs=(P("lev", None, MA, None), P(None, MA, None), P(), P()),
        out_specs=(P("lev", None, MA, None), P()),
        check_vma=False,
    )
```

```python
import jax
import jax.numpy as jnp
from jax import lax
from jax.experimental import pallas as pl
from jax.experimental.pallas import tpu as pltpu
from jax.experimental.layout import Layout, with_layout_constraint
from jax.sharding import Mesh
from jax.sharding import PartitionSpec as P

LEV = 72
WAVES = 1280
OWNERS = 64
FOLDS = 20
TILES = 10
HALF = 112
QROWS = 56
OWN = 18
STEP = 9
MA = ("ma_0", "ma_1", "ma_2")
F32 = jnp.float32
VMEM = pl.BlockSpec(memory_space=pltpu.VMEM)
SMEM = pl.BlockSpec(memory_space=pltpu.SMEM)
FAR = pl.BlockSpec(memory_space=pl.ANY)
QUARTER = jax.ShapeDtypeStruct((OWN, QROWS, 128), F32)


def in_vmem(x):
    return pltpu.with_memory_space_constraint(x, pltpu.VMEM)


def start_row(t):
    return 20 * t - t * (t - 1)


def cut(moves):
    out = []
    for s, d, n in moves:
        while n:
            step = min(n, QROWS - d % QROWS, QROWS - s % QROWS)
            out.append((s, d, step))
            s, d, n = s + step, d + step, n - step
    return out


def quarters(moves):
    out = []
    for s, d, n in moves:
        while n:
            step = min(n, QROWS - d % QROWS)
            out.append((s, d, step))
            s, d, n = s + step, d + step, n - step
    return out


LIVE = [((2 * t + par) * 20 + 2 * t, par * HALF + start_row(t), 20 - 2 * t) for par in range(2) for t in range(TILES)]
DOWN = cut(
    [(start_row(t + 1), HALF + start_row(t) + 2, 18 - 2 * t) for t in range(TILES - 1)]
    + [(HALF + start_row(t - 1) + 2, start_row(t), 20 - 2 * t) for t in range(1, TILES)]
)


PART = 3
PARTS = OWN // PART


def pack_kernel(x_ref, p_ref, x_buf, p_buf, in_sem, out_sem):
    own = [pl.ds(c * PART, PART) for c in range(PARTS)]
    loads = [pltpu.make_async_copy(x_ref.at[o], x_buf.at[o], in_sem.at[c]) for c, o in enumerate(own)]
    stores = [pltpu.make_async_copy(p_buf.at[:, o], p_ref.at[:, o], out_sem.at[c]) for c, o in enumerate(own)]
    for load in loads:
        load.start()
    for load, store, o in zip(loads, stores, own):
        load.wait()
        for s, d, n in quarters(LIVE):
            q, r = divmod(d, QROWS)
            p_buf[q, o, r : r + n, :] = x_buf[o, s : s + n, :]
        for q in (1, 3):
            p_buf[q, o, QROWS - 2 :, :] = jnp.zeros((PART, 2, 128), F32)
        store.start()
    for store in stores:
        store.wait()


def pack(x):
    packed = (4, OWN, QROWS, 128)
    return pl.pallas_call(
        pack_kernel,
        out_shape=jax.ShapeDtypeStruct(packed, F32),
        in_specs=[FAR],
        out_specs=FAR,
        scratch_shapes=[
            pltpu.VMEM(x.shape, F32),
            pltpu.VMEM(packed, F32),
            pltpu.SemaphoreType.DMA((PARTS,)),
            pltpu.SemaphoreType.DMA((PARTS,)),
        ],
        name="pack",
    )(x)


def as_rows(x):
    tiles = with_layout_constraint(x.reshape(OWN, 2, FOLDS, TILES, 128), Layout(major_to_minor=(0, 2, 3, 1, 4)))
    return tiles.transpose(0, 2, 3, 1, 4).reshape(OWN, 400, 128)


def from_rows(rows):
    tiles = rows.reshape(OWN, FOLDS, TILES, 2, 128).transpose(0, 3, 1, 2, 4)
    tiles = with_layout_constraint(tiles, Layout(major_to_minor=(0, 2, 3, 1, 4)))
    return tiles.reshape(OWN, 2, FOLDS, WAVES)


BASES = (1, 2, -2, -1)
PLACE = {-2: 0, -1: 1, 1: 2, 2: 3}


def prep_kernel(info, c_ref, h_ref, ck_ref, hp_ref, live_ref):
    owner = info[0]
    odd = info[1]
    for par in range(2):
        for t in range(TILES):
            fold = 2 * t + par
            n = TILES - t
            at = par * HALF + start_row(t)
            wave = fold * OWNERS + (owner if par == 0 else OWNERS - 1 - owner)
            col = lax.broadcasted_iota(jnp.int32, (n, 128), 0) * 128 + lax.broadcasted_iota(jnp.int32, (n, 128), 1) + 128 * t
            live = jnp.where(col >= wave, 1.0, 0.0).astype(F32)
            h = h_ref[t:TILES, :]
            for part in range(2):
                live_ref[pl.ds(at + part, n, stride=2), :] = live
                hp_ref[pl.ds(at + part, n, stride=2), :] = h
            for a, base in enumerate(BASES):
                s_even = base * (1 if par == 0 else -1)
                shift = jnp.where(odd == 1, -s_even, s_even)
                place = jnp.where(odd == 1, PLACE[-s_even], PLACE[s_even])
                low = jnp.where(wave + shift < 0, 2 * WAVES, jnp.maximum(wave, wave + shift))
                c = c_ref[pl.ds((fold * TILES + t) * 4 + place, n, stride=4), :]
                c = jnp.where(col >= low, c, 0.0)
                for part in range(2):
                    ck_ref[a, pl.ds(at + part, n, stride=2), :] = c
        pad = pl.ds(par * HALF + 110, 2)
        zero = jnp.zeros((2, 128), F32)
        live_ref[pad, :] = zero
        hp_ref[pad, :] = zero
        for a in range(4):
            ck_ref[a, pad, :] = zero


def prep(info, c, h):
    rows = jax.ShapeDtypeStruct((2 * HALF, 128), F32)
    vmem = pl.BlockSpec(memory_space=pltpu.VMEM)
    return pl.pallas_call(
        prep_kernel,
        out_shape=(jax.ShapeDtypeStruct((4, 2 * HALF, 128), F32), rows, rows),
        in_specs=[pl.BlockSpec(memory_space=pltpu.SMEM), vmem, vmem],
        out_specs=(vmem, vmem, vmem),
        name="prep",
    )(info, c, h)


ROWS = 24


def mix_kernel(info, w_ref, h_ref, *refs):
    x_ref, *outs = refs
    w = w_ref[:, : 3 * LEV].astype(jnp.bfloat16)
    d = w_ref[:LEV, 3 * LEV :]
    x2 = x_ref.reshape(LEV * QROWS, 128)
    for r in range(0, QROWS, 2):
        h = h_ref[0, r : r + 1, :]
        scale = 1.0 / (1.0 + h * d)
        highs, lows = [], []
        for e in range(2):
            f = x2[pl.ds(r + e, LEV, stride=QROWS), :] * scale
            high = f.astype(jnp.bfloat16).astype(F32)
            highs.append(high)
            lows.append(f - high)
        high = jnp.concatenate(highs, axis=1)
        low = jnp.concatenate(lows, axis=1)
        both = jnp.concatenate([high, high, low], axis=0).astype(jnp.bfloat16)
        out = jnp.dot(w, both, preferred_element_type=F32)
        for away, ref in enumerate(outs):
            o2 = ref.reshape(OWN * QROWS, 128)
            for e in range(2):
                part = out[away * ROWS : away * ROWS + OWN, e * 128 : (e + 1) * 128]
                o2[pl.ds(r + e, OWN, stride=QROWS), :] = part * h


def mix(info, w3, hp, x):
    held = pl.BlockSpec((OWN, QROWS, 128), lambda i, s: (0, 0, 0))
    return pl.pallas_call(
        mix_kernel,
        out_shape=[QUARTER] * 4,
        grid_spec=pltpu.PrefetchScalarGridSpec(
            num_scalar_prefetch=1,
            grid=(1,),
            in_specs=[
                pl.BlockSpec((4 * ROWS, 3 * LEV + 1), lambda i, s: (0, 0)),
                pl.BlockSpec((1, QROWS, 128), lambda i, s: (s[2], 0, 0)),
                VMEM,
            ],
            out_specs=[held] * 4,
        ),
        name="mix",
    )(info, w3, hp, in_vmem(x))


def mix_table(vertical, lev):
    diag = jnp.sum(vertical * jnp.eye(LEV, dtype=F32), axis=1)
    padded = jnp.pad(vertical.reshape(4, OWN, LEV), ((0, 0), (0, ROWS - OWN), (0, 0))).reshape(4 * ROWS, LEV)
    turned = lax.dynamic_slice_in_dim(jnp.concatenate([padded, padded], axis=0), lev * ROWS, 4 * ROWS, 0)
    high = lax.reduce_precision(turned, 8, 7)
    column = jnp.pad(diag[:, None], ((0, 4 * ROWS - LEV), (0, 0)))
    return diag, jnp.concatenate([high, turned - high, high, column], axis=1)


def fold_sum(acc, slot, value):
    acc[slot] += jnp.sum((value * value).reshape(QROWS // 8, 8, 128), axis=0)


def near_kernel(info, d_ref, ck_ref, hp_ref, live_ref, p_ref, q_ref, x_ref, y_ref, z_ref, o_ref, kept_ref, s_ref, fix):
    step = pl.program_id(0)
    received = (x_ref, y_ref, z_ref)

    @pl.when(step == 0)
    def _():
        s_ref[...] = jnp.zeros_like(s_ref)

    def every(get):
        def chunk(c, _):
            rows = pl.ds(pl.multiple_of(c * 8, 8), 8)
            for q in range(4):
                live, hp = live_ref[q, rows, :], hp_ref[q, rows, :]
                ck = [ck_ref[a, q, rows, :] for a in range(4)]
                squares = jnp.zeros((8, 128), F32)
                for l in range(STEP):
                    scale = 1.0 / (1.0 + hp * d_ref[info[2] * OWN + step * STEP + l])
                    v = p_ref[q, l, rows, :] * live
                    near = ck[0] * q_ref[q, l, rows, :] + v
                    for a in range(3):
                        near = near + ck[a + 1] * get(a, q, l, rows)
                    left = v - scale * near * live
                    o_ref[q, l, rows, :] = left
                    kept_ref[q, step * STEP + l, rows, :] = left
                    squares = squares + v * v
                s_ref[0] += squares
            return 0

        lax.fori_loop(0, QROWS // 8, chunk, 0)

    @pl.when(info[0] > 1)
    def _():
        every(lambda a, q, l, rows: received[a][jnp.where(info[3 + a] == 1, q ^ 2, q), l, rows, :])

    @pl.when(info[0] <= 1)
    def _():
        for a in range(3):

            @pl.when(info[3 + a] == 2)
            def _():
                fix[a] = jnp.zeros(fix.shape[1:], F32)
                for s, t, n in DOWN:
                    fix[a, t // QROWS, :, t % QROWS : t % QROWS + n, :] = received[a][s // QROWS, :, s % QROWS : s % QROWS + n, :]

            @pl.when(info[3 + a] != 2)
            def _():
                fix[a] = received[a][...]

        every(lambda a, q, l, rows: fix[a, q, l, rows, :])


def whole(shape):
    return pl.BlockSpec(shape, lambda i, s: (0,) * len(shape))


BLOCK = pl.BlockSpec((4, STEP, QROWS, 128), lambda i, s: (0, i, 0, 0))
SUM = jax.ShapeDtypeStruct((1, 8, 128), F32)


def near(info, diag, ck, hp, live, p, q, x, y, z):
    return pl.pallas_call(
        near_kernel,
        out_shape=(jax.ShapeDtypeStruct(p.shape, F32), pltpu.VMEM(p.shape, F32), SUM),
        grid_spec=pltpu.PrefetchScalarGridSpec(
            num_scalar_prefetch=1,
            grid=(OWN // STEP,),
            in_specs=[SMEM, whole((4, 4, QROWS, 128)), whole((4, QROWS, 128)), whole((4, QROWS, 128))] + [BLOCK] * 5,
            out_specs=[BLOCK, VMEM, whole((1, 8, 128))],
            scratch_shapes=[pltpu.VMEM((3, 4, STEP, QROWS, 128), F32)],
        ),
        name="near",
    )(info, diag, ck, hp, live, p, q, x, y, z)


def finish_kernel(base, info, d_ref, hp_ref, live_ref, p_ref, part_ref, *refs):
    o_ref, buf = refs[-2:]
    step = base // FINISH_STEP + pl.program_id(0)
    for l in range(FINISH_STEP):
        d = d_ref[info[2] * OWN + step * FINISH_STEP + l]
        for away in range(4):
            q = (info[2] - away) & 3
            live = live_ref[q]
            scale = 1.0 / (1.0 + hp_ref[q] * d)
            residual = part_ref[q, l] - refs[away][l] * live
            buf[l, pl.ds(pl.multiple_of(q * QROWS, 8), QROWS), :] = scale * (p_ref[q, l] * live + residual)
    for s, d, n in LIVE:
        if n < 20:
            o_ref[:, s + n - 20 : s, :] = jnp.zeros((FINISH_STEP, 20 - n, 128), F32)
        o_ref[:, s : s + n, :] = buf[:, d : d + n, :]


def finish(base, info, diag, hp, live, p, part, m, *before):
    at = base // FINISH_STEP
    block = pl.BlockSpec((4, FINISH_STEP, QROWS, 128), lambda i, s: (0, i + at, 0, 0))
    piece = pl.BlockSpec((FINISH_STEP, QROWS, 128), lambda i, s: (i + at, 0, 0))
    return pl.pallas_call(
        lambda *refs: finish_kernel(base, *refs),
        out_shape=jax.ShapeDtypeStruct((OWN, 400, 128), F32),
        grid_spec=pltpu.PrefetchScalarGridSpec(
            num_scalar_prefetch=1,
            grid=(OWN // 2 // FINISH_STEP,),
            in_specs=[SMEM, whole((4, QROWS, 128)), whole((4, QROWS, 128))]
            + [block] * 2
            + [piece] * 4
            + [pl.BlockSpec(memory_space=pl.ANY)] * len(before),
            out_specs=pl.BlockSpec((FINISH_STEP, 400, 128), lambda i, s: (i + at, 0, 0)),
            scratch_shapes=[pltpu.VMEM((FINISH_STEP, 2 * HALF, 128), F32)],
        ),
        input_output_aliases={10: 0} if before else {},
        name="finish",
    )(info, diag, hp, live, p, part, *m, *before)


def squares_kernel(info, v_ref, live_ref, part_ref, *refs):
    o_ref, acc = refs[-2:]
    step = pl.program_id(0)

    @pl.when(step == 0)
    def _():
        acc[...] = jnp.zeros_like(acc)

    def chunk(c, _):
        rows = pl.ds(pl.multiple_of(c * 8, 8), 8)
        sums = [jnp.zeros((8, 128), F32) for _ in range(8)]
        for away in range(4):
            q = (info[2] - away) & 3
            live = live_ref[q, rows, :]
            for l in range(SQUARES_STEP):
                residual = part_ref[q, step * SQUARES_STEP + l, rows, :] - refs[away][l, rows, :] * live
                sums[2 * away + l % 2] += residual * residual
        while len(sums) > 1:
            sums = [a + b for a, b in zip(sums[::2], sums[1::2])]
        acc[0] += sums[0]
        return 0

    lax.fori_loop(0, QROWS // 8, chunk, 0)

    @pl.when(step == pl.num_programs(0) - 1)
    def _():
        row = lax.broadcasted_iota(jnp.int32, (8, 128), 0)
        both = jnp.where(row == 0, jnp.sum(v_ref[0]), jnp.sum(acc[0]))
        o_ref[...] = jnp.broadcast_to(both, o_ref.shape)


SQUARES_STEP = 9
FINISH_STEP = 9


def squares(copies, info, v_sum, live, part, m):
    piece = pl.BlockSpec((SQUARES_STEP, QROWS, 128), lambda i, s: (i, 0, 0))
    return pl.pallas_call(
        squares_kernel,
        out_shape=jax.ShapeDtypeStruct((copies, 8, 128), F32),
        grid_spec=pltpu.PrefetchScalarGridSpec(
            num_scalar_prefetch=1,
            grid=(OWN // SQUARES_STEP,),
            in_specs=[whole((1, 8, 128)), whole((4, QROWS, 128)), VMEM] + [piece] * 4,
            out_specs=whole((copies, 8, 128)),
            scratch_shapes=[pltpu.VMEM((1, 8, 128), F32)],
        ),
        name="squares",
    )(info, v_sum, live, in_vmem(part), *m)


def routes(owners):
    x, y = [], []
    for o in range(owners):
        down = o - 2 if o >= 2 else 1 - o
        up = o + 2 if o + 2 < owners else 2 * owners - 1 - (o + 2)
        x.append((o, down if o % 2 == 0 else up))
        y.append((o, up if o % 2 == 0 else down))
    return x, y, [(o, o ^ 1) for o in range(owners)]


def total(copies, axes):
    return jnp.sum(lax.all_to_all(copies, axes, 0, 0, tiled=True), axis=0)


def body(forcing, coupling, helmholtz, vertical):
    owner = lax.axis_index(MA).astype(jnp.int32)
    lev = lax.axis_index("lev").astype(jnp.int32)
    ends = {"x": (1, OWNERS - 2), "y": (0, OWNERS - 1), "z": (0, OWNERS - 1)}
    modes = [jnp.where(owner == low, 2, jnp.where(owner == high, 1, 0)) for low, high in ends.values()]
    info = jnp.stack([owner, owner & 1, lev] + modes).astype(jnp.int32)
    crows = coupling.reshape(4, FOLDS, TILES, 128).transpose(1, 2, 0, 3).reshape(800, 128)
    p = pack(as_rows(forcing))
    to_x, to_y, swap = routes(OWNERS)
    along = lambda v, away: lax.ppermute(v, "lev", [(i, (i + away) % 4) for i in range(4)])
    every = lax.all_to_all(p, "lev", 0, 0, tiled=True).reshape(LEV, QROWS, 128)
    x = lax.ppermute(p, MA, to_x)
    q = lax.ppermute(p, MA, swap)
    ck, hp, live = prep(info, crows, helmholtz.reshape(TILES, 128))
    diag, w3 = mix_table(vertical, lev)
    x, p_after, ck, hp, live, w3 = lax.optimization_barrier((x, p, ck, hp, live, w3))
    y = lax.ppermute(p_after, MA, to_y)
    z = lax.ppermute(x, MA, swap)
    ck = ck.reshape(4, 4, QROWS, 128)
    hp = hp.reshape(4, QROWS, 128)
    live = live.reshape(4, QROWS, 128)
    mixed = mix(info, w3, hp, every)
    m = [mixed[0]] + [along(v, away) for v, away in zip(mixed[1:], (1, 2, 3))]
    part, kept, v_sum = near(info, diag, ck, hp, live, p, q, x, y, z)
    part, *m = lax.optimization_barrier((part, *m))
    inner, outer = ("ma_1", "ma_2"), ("ma_0", "lev")
    sums = total(squares(lax.axis_size(inner), info, v_sum, live, kept, m), inner)
    rows = finish(0, info, diag, hp, live, p, part, m)
    sums, rows = lax.optimization_barrier((sums, rows))
    sums = total(jnp.broadcast_to(sums[None], (lax.axis_size(outer), 8, 128)), outer)
    rows = finish(OWN // 2, info, diag, hp, live, p, part, m, rows)
    norms = jnp.sqrt(sums[:2, 0] / (LEV * WAVES * (WAVES + 1)))
    return (from_rows(rows), norms)


def solution(mesh):
    split = Mesh(mesh.devices.reshape(4, 8, 2, mesh.shape["lev"]), ("ma_0", "ma_1", "ma_2", "lev"))
    return jax.shard_map(
        body,
        mesh=split,
        in_specs=(P("lev", None, MA, None), P(None, MA, None), P(), P()),
        out_specs=(P("lev", None, MA, None), P()),
        check_vma=False,
    )
```

```python
import jax
import jax.numpy as jnp
from jax import lax
from jax.experimental import pallas as pl
from jax.experimental.pallas import tpu as pltpu
from jax.experimental.layout import Layout, with_layout_constraint
from jax.sharding import Mesh
from jax.sharding import PartitionSpec as P

LEV = 72
WAVES = 1280
OWNERS = 64
FOLDS = 20
TILES = 10
HALF = 112
QROWS = 56
OWN = 18
STEP = 9
MA = ("ma_0", "ma_1", "ma_2")
F32 = jnp.float32
VMEM = pl.BlockSpec(memory_space=pltpu.VMEM)
SMEM = pl.BlockSpec(memory_space=pltpu.SMEM)
FAR = pl.BlockSpec(memory_space=pl.ANY)
QUARTER = jax.ShapeDtypeStruct((OWN, QROWS, 128), F32)


def in_vmem(x):
    return pltpu.with_memory_space_constraint(x, pltpu.VMEM)


def start_row(t):
    return 20 * t - t * (t - 1)


def cut(moves):
    out = []
    for s, d, n in moves:
        while n:
            step = min(n, QROWS - d % QROWS, QROWS - s % QROWS)
            out.append((s, d, step))
            s, d, n = s + step, d + step, n - step
    return out


def quarters(moves):
    out = []
    for s, d, n in moves:
        while n:
            step = min(n, QROWS - d % QROWS)
            out.append((s, d, step))
            s, d, n = s + step, d + step, n - step
    return out


LIVE = [((2 * t + par) * 20 + 2 * t, par * HALF + start_row(t), 20 - 2 * t) for par in range(2) for t in range(TILES)]
DOWN = cut(
    [(start_row(t + 1), HALF + start_row(t) + 2, 18 - 2 * t) for t in range(TILES - 1)]
    + [(HALF + start_row(t - 1) + 2, start_row(t), 20 - 2 * t) for t in range(1, TILES)]
)


PART = 3
PARTS = OWN // PART


def pack_kernel(x_ref, p_ref, x_buf, p_buf, in_sem, out_sem):
    own = [pl.ds(c * PART, PART) for c in range(PARTS)]
    loads = [pltpu.make_async_copy(x_ref.at[o], x_buf.at[o], in_sem.at[c]) for c, o in enumerate(own)]
    stores = [pltpu.make_async_copy(p_buf.at[:, o], p_ref.at[:, o], out_sem.at[c]) for c, o in enumerate(own)]
    for load in loads:
        load.start()
    for load, store, o in zip(loads, stores, own):
        load.wait()
        for s, d, n in quarters(LIVE):
            q, r = divmod(d, QROWS)
            p_buf[q, o, r : r + n, :] = x_buf[o, s : s + n, :]
        for q in (1, 3):
            p_buf[q, o, QROWS - 2 :, :] = jnp.zeros((PART, 2, 128), F32)
        store.start()
    for store in stores:
        store.wait()


def pack(x):
    packed = (4, OWN, QROWS, 128)
    return pl.pallas_call(
        pack_kernel,
        out_shape=jax.ShapeDtypeStruct(packed, F32),
        in_specs=[FAR],
        out_specs=FAR,
        scratch_shapes=[
            pltpu.VMEM(x.shape, F32),
            pltpu.VMEM(packed, F32),
            pltpu.SemaphoreType.DMA((PARTS,)),
            pltpu.SemaphoreType.DMA((PARTS,)),
        ],
        name="pack",
    )(x)


def as_rows(x):
    tiles = with_layout_constraint(x.reshape(OWN, 2, FOLDS, TILES, 128), Layout(major_to_minor=(0, 2, 3, 1, 4)))
    return tiles.transpose(0, 2, 3, 1, 4).reshape(OWN, 400, 128)


def from_rows(rows):
    tiles = rows.reshape(OWN, FOLDS, TILES, 2, 128).transpose(0, 3, 1, 2, 4)
    tiles = with_layout_constraint(tiles, Layout(major_to_minor=(0, 2, 3, 1, 4)))
    return tiles.reshape(OWN, 2, FOLDS, WAVES)


BASES = (1, 2, -2, -1)
PLACE = {-2: 0, -1: 1, 1: 2, 2: 3}


def prep_kernel(info, c_ref, h_ref, ck_ref, hp_ref, live_ref):
    owner = info[0]
    odd = info[1]
    for par in range(2):
        for t in range(TILES):
            fold = 2 * t + par
            n = TILES - t
            at = par * HALF + start_row(t)
            wave = fold * OWNERS + (owner if par == 0 else OWNERS - 1 - owner)
            col = lax.broadcasted_iota(jnp.int32, (n, 128), 0) * 128 + lax.broadcasted_iota(jnp.int32, (n, 128), 1) + 128 * t
            live = jnp.where(col >= wave, 1.0, 0.0).astype(F32)
            h = h_ref[t:TILES, :]
            for part in range(2):
                live_ref[pl.ds(at + part, n, stride=2), :] = live
                hp_ref[pl.ds(at + part, n, stride=2), :] = h
            for a, base in enumerate(BASES):
                s_even = base * (1 if par == 0 else -1)
                shift = jnp.where(odd == 1, -s_even, s_even)
                place = jnp.where(odd == 1, PLACE[-s_even], PLACE[s_even])
                low = jnp.where(wave + shift < 0, 2 * WAVES, jnp.maximum(wave, wave + shift))
                c = c_ref[pl.ds((fold * TILES + t) * 4 + place, n, stride=4), :]
                c = jnp.where(col >= low, c, 0.0)
                for part in range(2):
                    ck_ref[a, pl.ds(at + part, n, stride=2), :] = c
        pad = pl.ds(par * HALF + 110, 2)
        zero = jnp.zeros((2, 128), F32)
        live_ref[pad, :] = zero
        hp_ref[pad, :] = zero
        for a in range(4):
            ck_ref[a, pad, :] = zero


def prep(info, c, h):
    rows = jax.ShapeDtypeStruct((2 * HALF, 128), F32)
    vmem = pl.BlockSpec(memory_space=pltpu.VMEM)
    return pl.pallas_call(
        prep_kernel,
        out_shape=(jax.ShapeDtypeStruct((4, 2 * HALF, 128), F32), rows, rows),
        in_specs=[pl.BlockSpec(memory_space=pltpu.SMEM), vmem, vmem],
        out_specs=(vmem, vmem, vmem),
        name="prep",
    )(info, c, h)


ROWS = 24


def mix_kernel(info, w_ref, h_ref, *refs):
    x_ref, far_outs, outs, sem = refs[0], refs[1:5], refs[5:9], refs[9]
    ends = (0, 32, QROWS)
    stores = [
        [pltpu.make_async_copy(o.at[:, a:b], far.at[:, a:b], sem.at[i, k]) for i, (o, far) in enumerate(zip(outs, far_outs))]
        for k, (a, b) in enumerate(zip(ends, ends[1:]))
    ]
    w = w_ref[:, : 3 * LEV].astype(jnp.bfloat16)
    d = w_ref[:LEV, 3 * LEV :]
    x2 = x_ref.reshape(LEV * QROWS, 128)
    for r in range(0, QROWS, 2):
        h = h_ref[0, r : r + 1, :]
        scale = 1.0 / (1.0 + h * d)
        highs, lows = [], []
        for e in range(2):
            f = x2[pl.ds(r + e, LEV, stride=QROWS), :] * scale
            high = f.astype(jnp.bfloat16).astype(F32)
            highs.append(high)
            lows.append(f - high)
        high = jnp.concatenate(highs, axis=1)
        low = jnp.concatenate(lows, axis=1)
        both = jnp.concatenate([high, high, low], axis=0).astype(jnp.bfloat16)
        out = jnp.dot(w, both, preferred_element_type=F32)
        for away, ref in enumerate(outs):
            o2 = ref.reshape(OWN * QROWS, 128)
            for e in range(2):
                part = out[away * ROWS : away * ROWS + OWN, e * 128 : (e + 1) * 128]
                o2[pl.ds(r + e, OWN, stride=QROWS), :] = part * h
        if r + 2 in ends:
            for store in stores[ends.index(r + 2) - 1]:
                store.start()
    for store in stores[0] + stores[1]:
        store.wait()


def mix(info, w3, hp, x):
    return pl.pallas_call(
        mix_kernel,
        out_shape=[QUARTER] * 4,
        grid_spec=pltpu.PrefetchScalarGridSpec(
            num_scalar_prefetch=1,
            grid=(1,),
            in_specs=[
                pl.BlockSpec((4 * ROWS, 3 * LEV + 1), lambda i, s: (0, 0)),
                pl.BlockSpec((1, QROWS, 128), lambda i, s: (s[2], 0, 0)),
                VMEM,
            ],
            out_specs=[FAR] * 4,
            scratch_shapes=[pltpu.VMEM((OWN, QROWS, 128), F32)] * 4 + [pltpu.SemaphoreType.DMA((4, 2))],
        ),
        name="mix",
    )(info, w3, hp, in_vmem(x))


def mix_table(vertical, lev):
    diag = jnp.sum(vertical * jnp.eye(LEV, dtype=F32), axis=1)
    padded = jnp.pad(vertical.reshape(4, OWN, LEV), ((0, 0), (0, ROWS - OWN), (0, 0))).reshape(4 * ROWS, LEV)
    turned = lax.dynamic_slice_in_dim(jnp.concatenate([padded, padded], axis=0), lev * ROWS, 4 * ROWS, 0)
    high = lax.reduce_precision(turned, 8, 7)
    column = jnp.pad(diag[:, None], ((0, 4 * ROWS - LEV), (0, 0)))
    return diag, jnp.concatenate([high, turned - high, high, column], axis=1)


def fold_sum(acc, slot, value):
    acc[slot] += jnp.sum((value * value).reshape(QROWS // 8, 8, 128), axis=0)


def near_kernel(info, d_ref, ck_ref, hp_ref, live_ref, p_ref, q_ref, x_ref, y_ref, z_ref, o_ref, kept_ref, s_ref, fix):
    step = pl.program_id(0)
    received = (x_ref, y_ref, z_ref)

    @pl.when(step == 0)
    def _():
        s_ref[...] = jnp.zeros_like(s_ref)

    def every(get):
        def chunk(c, _):
            rows = pl.ds(pl.multiple_of(c * 8, 8), 8)
            for q in range(4):
                live, hp = live_ref[q, rows, :], hp_ref[q, rows, :]
                ck = [ck_ref[a, q, rows, :] for a in range(4)]
                squares = jnp.zeros((8, 128), F32)
                for l in range(STEP):
                    scale = 1.0 / (1.0 + hp * d_ref[info[2] * OWN + step * STEP + l])
                    v = p_ref[q, l, rows, :] * live
                    near = ck[0] * q_ref[q, l, rows, :] + v
                    for a in range(3):
                        near = near + ck[a + 1] * get(a, q, l, rows)
                    left = v - scale * near * live
                    o_ref[q, l, rows, :] = left
                    kept_ref[q, step * STEP + l, rows, :] = left
                    squares = squares + v * v
                s_ref[0] += squares
            return 0

        lax.fori_loop(0, QROWS // 8, chunk, 0)

    @pl.when(info[0] > 1)
    def _():
        every(lambda a, q, l, rows: received[a][jnp.where(info[3 + a] == 1, q ^ 2, q), l, rows, :])

    @pl.when(info[0] <= 1)
    def _():
        for a in range(3):

            @pl.when(info[3 + a] == 2)
            def _():
                fix[a] = jnp.zeros(fix.shape[1:], F32)
                for s, t, n in DOWN:
                    fix[a, t // QROWS, :, t % QROWS : t % QROWS + n, :] = received[a][s // QROWS, :, s % QROWS : s % QROWS + n, :]

            @pl.when(info[3 + a] != 2)
            def _():
                fix[a] = received[a][...]

        every(lambda a, q, l, rows: fix[a, q, l, rows, :])


def whole(shape):
    return pl.BlockSpec(shape, lambda i, s: (0,) * len(shape))


BLOCK = pl.BlockSpec((4, STEP, QROWS, 128), lambda i, s: (0, i, 0, 0))
SUM = jax.ShapeDtypeStruct((1, 8, 128), F32)


def near(info, diag, ck, hp, live, p, q, x, y, z):
    return pl.pallas_call(
        near_kernel,
        out_shape=(jax.ShapeDtypeStruct(p.shape, F32), pltpu.VMEM(p.shape, F32), SUM),
        grid_spec=pltpu.PrefetchScalarGridSpec(
            num_scalar_prefetch=1,
            grid=(OWN // STEP,),
            in_specs=[SMEM, whole((4, 4, QROWS, 128)), whole((4, QROWS, 128)), whole((4, QROWS, 128))] + [BLOCK] * 5,
            out_specs=[BLOCK, VMEM, whole((1, 8, 128))],
            scratch_shapes=[pltpu.VMEM((3, 4, STEP, QROWS, 128), F32)],
        ),
        name="near",
    )(info, diag, ck, hp, live, p, q, x, y, z)


def finish_kernel(base, info, d_ref, hp_ref, live_ref, p_ref, part_ref, *refs):
    o_ref, buf = refs[-2:]
    step = base // FINISH_STEP + pl.program_id(0)
    for l in range(FINISH_STEP):
        d = d_ref[info[2] * OWN + step * FINISH_STEP + l]
        for away in range(4):
            q = (info[2] - away) & 3
            live = live_ref[q]
            scale = 1.0 / (1.0 + hp_ref[q] * d)
            residual = part_ref[q, l] - refs[away][l] * live
            buf[l, pl.ds(pl.multiple_of(q * QROWS, 8), QROWS), :] = scale * (p_ref[q, l] * live + residual)
    for s, d, n in LIVE:
        if n < 20:
            o_ref[:, s + n - 20 : s, :] = jnp.zeros((FINISH_STEP, 20 - n, 128), F32)
        o_ref[:, s : s + n, :] = buf[:, d : d + n, :]


def finish(base, info, diag, hp, live, p, part, m, *before):
    at = base // FINISH_STEP
    block = pl.BlockSpec((4, FINISH_STEP, QROWS, 128), lambda i, s: (0, i + at, 0, 0))
    piece = pl.BlockSpec((FINISH_STEP, QROWS, 128), lambda i, s: (i + at, 0, 0))
    return pl.pallas_call(
        lambda *refs: finish_kernel(base, *refs),
        out_shape=jax.ShapeDtypeStruct((OWN, 400, 128), F32),
        grid_spec=pltpu.PrefetchScalarGridSpec(
            num_scalar_prefetch=1,
            grid=(OWN // 2 // FINISH_STEP,),
            in_specs=[SMEM, whole((4, QROWS, 128)), whole((4, QROWS, 128))]
            + [block] * 2
            + [piece] * 4
            + [pl.BlockSpec(memory_space=pl.ANY)] * len(before),
            out_specs=pl.BlockSpec((FINISH_STEP, 400, 128), lambda i, s: (i + at, 0, 0)),
            scratch_shapes=[pltpu.VMEM((FINISH_STEP, 2 * HALF, 128), F32)],
        ),
        input_output_aliases={10: 0} if before else {},
        name="finish",
    )(info, diag, hp, live, p, part, *m, *before)


def squares_kernel(info, v_ref, live_ref, part_ref, *refs):
    o_ref, acc = refs[-2:]
    step = pl.program_id(0)

    @pl.when(step == 0)
    def _():
        acc[...] = jnp.zeros_like(acc)

    def chunk(c, _):
        rows = pl.ds(pl.multiple_of(c * 8, 8), 8)
        sums = [jnp.zeros((8, 128), F32) for _ in range(8)]
        for away in range(4):
            q = (info[2] - away) & 3
            live = live_ref[q, rows, :]
            for l in range(SQUARES_STEP):
                residual = part_ref[q, step * SQUARES_STEP + l, rows, :] - refs[away][l, rows, :] * live
                sums[2 * away + l % 2] += residual * residual
        while len(sums) > 1:
            sums = [a + b for a, b in zip(sums[::2], sums[1::2])]
        acc[0] += sums[0]
        return 0

    lax.fori_loop(0, QROWS // 8, chunk, 0)

    @pl.when(step == pl.num_programs(0) - 1)
    def _():
        lane = lax.broadcasted_iota(jnp.int32, (1, 128), 1)
        both = jnp.where(lane < 64, jnp.sum(v_ref[0]), jnp.sum(acc[0]))
        o_ref[...] = jnp.broadcast_to(both, o_ref.shape)


SQUARES_STEP = 9
FINISH_STEP = 9


def squares(copies, info, v_sum, live, part, m):
    piece = pl.BlockSpec((SQUARES_STEP, QROWS, 128), lambda i, s: (i, 0, 0))
    return pl.pallas_call(
        squares_kernel,
        out_shape=jax.ShapeDtypeStruct((copies, 1, 128), F32),
        grid_spec=pltpu.PrefetchScalarGridSpec(
            num_scalar_prefetch=1,
            grid=(OWN // SQUARES_STEP,),
            in_specs=[whole((1, 8, 128)), whole((4, QROWS, 128)), VMEM] + [piece] * 4,
            out_specs=whole((copies, 1, 128)),
            scratch_shapes=[pltpu.VMEM((1, 8, 128), F32)],
        ),
        name="squares",
    )(info, v_sum, live, in_vmem(part), *m)


def routes(owners):
    x, y = [], []
    for o in range(owners):
        down = o - 2 if o >= 2 else 1 - o
        up = o + 2 if o + 2 < owners else 2 * owners - 1 - (o + 2)
        x.append((o, down if o % 2 == 0 else up))
        y.append((o, up if o % 2 == 0 else down))
    return x, y, [(o, o ^ 1) for o in range(owners)]


def total(copies, axes):
    return jnp.sum(lax.all_to_all(copies, axes, 0, 0, tiled=True), axis=0)


def body(forcing, coupling, helmholtz, vertical):
    owner = lax.axis_index(MA).astype(jnp.int32)
    lev = lax.axis_index("lev").astype(jnp.int32)
    ends = {"x": (1, OWNERS - 2), "y": (0, OWNERS - 1), "z": (0, OWNERS - 1)}
    modes = [jnp.where(owner == low, 2, jnp.where(owner == high, 1, 0)) for low, high in ends.values()]
    info = jnp.stack([owner, owner & 1, lev] + modes).astype(jnp.int32)
    crows = coupling.reshape(4, FOLDS, TILES, 128).transpose(1, 2, 0, 3).reshape(800, 128)
    p = pack(as_rows(forcing))
    to_x, to_y, swap = routes(OWNERS)
    along = lambda v, away: lax.ppermute(v, "lev", [(i, (i + away) % 4) for i in range(4)])
    every = lax.all_to_all(p, "lev", 0, 0, tiled=True).reshape(LEV, QROWS, 128)
    x = lax.ppermute(p, MA, to_x)
    q = lax.ppermute(p, MA, swap)
    ck, hp, live = prep(info, crows, helmholtz.reshape(TILES, 128))
    diag, w3 = mix_table(vertical, lev)
    x, p_after, ck, hp, live, w3 = lax.optimization_barrier((x, p, ck, hp, live, w3))
    y = lax.ppermute(p_after, MA, to_y)
    z = lax.ppermute(x, MA, swap)
    ck = ck.reshape(4, 4, QROWS, 128)
    hp = hp.reshape(4, QROWS, 128)
    live = live.reshape(4, QROWS, 128)
    mixed = mix(info, w3, hp, every)
    m = [mixed[0]] + [along(v, away) for v, away in zip(mixed[1:], (1, 2, 3))]
    part, kept, v_sum = near(info, diag, ck, hp, live, p, q, x, y, z)
    part, *m = lax.optimization_barrier((part, *m))
    inner, outer = ("ma_1", "ma_2"), ("ma_0", "lev")
    sums = total(squares(lax.axis_size(inner), info, v_sum, live, kept, m), inner)
    rows = finish(0, info, diag, hp, live, p, part, m)
    sums, rows = lax.optimization_barrier((sums, rows))
    sums = total(jnp.broadcast_to(sums[None], (lax.axis_size(outer), 1, 128)), outer)
    rows = finish(OWN // 2, info, diag, hp, live, p, part, m, rows)
    norms = jnp.sqrt(sums[0, ::64] / (LEV * WAVES * (WAVES + 1)))
    return (from_rows(rows), norms)


def solution(mesh):
    split = Mesh(mesh.devices.reshape(4, 8, 2, mesh.shape["lev"]), ("ma_0", "ma_1", "ma_2", "lev"))
    return jax.shard_map(
        body,
        mesh=split,
        in_specs=(P("lev", None, MA, None), P(None, MA, None), P(), P()),
        out_specs=(P("lev", None, MA, None), P()),
        check_vma=False,
    )
```
